128 devices in a mesh: path: 16 (over y_hi, z, core), trade: 8 (over y_lo, x).
Axes of the slice: x: 4, y: 4 (y_hi: 2, y_lo: 2; y = y_hi * 2 + y_lo), z: 4, core: 2. Of those that a mesh axis runs over, the one named last changes fastest.
Arguments:
- state: bfloat16 [3, 16384, 128], P(None, 'path'), may hold values from -5 to 5
- basis_projection_weight: bfloat16 [128, 256], replicated, may hold values from -0.5 to 0.5
- factor_node_loading: bfloat16 [128, 1024], replicated, may hold values from -0.011962891 to 0.011962891
- curve: float32 [1024], replicated, may hold values from 0.01 to 0.05
- discount: float32 [3, 16384], P(None, 'path'), may hold values from 0.7 to 1
- region: int32 [3, 16384, 32], P(None, 'path', 'trade'), may hold values from 0 to 2
- carry_in: float32 [16384, 32], P('path', 'trade'), may hold values from -1.5 to 2.5
- group_of: int32 [20000], P('trade'), may hold values from 0 to 31, as said below
- swap_start: int32 [20000], P('trade'), may hold values from 0 to 511
- swap_length: int32 [20000], P('trade'), may hold values from 8 to 511
- strike: float32 [20000], P('trade'), may hold values from 0.01 to 0.05
- notional: float32 [20000], P('trade'), may hold values from -0.6 to 0.6
- bucket_map: float32 [1024, 64], replicated, may hold values from -0.1875 to 0.1875
Outputs:
- values: float32 [16384, 32], P('path', 'trade')
- coefficients: float32 [3, 32, 256], P(None, 'trade')
- node_adjoint: float32 [1024], replicated
- bucketed: float32 [64], replicated
The draws below stay inside these ranges and needn't reach their ends.
Inputs may be any that keep to these rules, and one draw needn't show every extreme that they name: `group_of`: trade t belongs to a group from (t // 2500) * 4 to (t // 2500) * 4 + 3.
All inputs are finite; a program needn't handle non-finite values.
Results may differ from the reference program's by a relative error of at most 0.005.
Values may be sent and summed in bfloat16 or wider, within the bound.
A program may use at most 128 MiB of HBM per device.

```python
import jax
import jax.numpy as jnp
from jax import lax

EXD = 3
BASIS = 256
NODES = 1024
FAC = 128
BUCKETS = 64
GRP_DEV = 4
TR_DEV = 2500
PATHS = 16384
TRADES = 20000
TRADE_GROUPS = 32


def draw_group_of(key, part):
    blocks = jnp.arange(TRADES, dtype=jnp.int32) // TR_DEV * GRP_DEV
    return (blocks + jax.random.randint(jax.random.fold_in(key, 11), (TRADES,), 0, GRP_DEV)).astype(jnp.int32)


def shared_state(key):
    centre_key = jax.random.fold_in(key, 101)
    noise_key = jax.random.fold_in(key, 102)
    centre = jax.random.uniform(centre_key, (FAC,), jnp.float32, -1.0, 1.0)
    noise = jnp.clip(jax.random.normal(noise_key, (EXD, PATHS, FAC), jnp.float32), -4.0, 4.0)
    return centre[None, None, :] + noise


def draw_state(key, part):
    return shared_state(key).astype(jnp.bfloat16)


def draw_carry_in(key, part):
    latest = shared_state(key)[EXD - 1]
    direction = jax.random.normal(jax.random.fold_in(key, 103), (FAC, TRADE_GROUPS), jnp.float32) / jnp.sqrt(jnp.float32(FAC))
    level = jax.random.uniform(jax.random.fold_in(key, 104), (TRADE_GROUPS,), jnp.float32, 0.2, 1.0)
    noise = 0.3 * jnp.clip(jax.random.normal(jax.random.fold_in(key, 105), (PATHS, TRADE_GROUPS), jnp.float32), -3.0, 3.0)
    smooth = jnp.tanh(jnp.dot(latest, direction, precision=lax.Precision.HIGHEST))
    return (0.6 * smooth + level[None, :] + noise).astype(jnp.float32)


def set_ends(values, rng, smallest, largest):
    place = [jax.random.randint(jax.random.fold_in(rng, axis), (), 0, length) for axis, length in enumerate(values.shape)]
    longest = values.shape.index(max(values.shape))
    next_to = place[:longest] + [(place[longest] + 1) % values.shape[longest]] + place[longest + 1:]
    return values.at[tuple(place)].set(smallest).at[tuple(next_to)].set(largest)


def block_scale(key, shape, shards, low, high):
    factor_of = 1.0
    for dim, shards_of in shards:
        heights = jax.random.uniform(jax.random.fold_in(jax.random.fold_in(key, 6), dim), (shards_of,), jnp.float32, low / len(shards), high / len(shards))
        factor_of = factor_of * jnp.repeat(jnp.exp(heights), shape[dim] // shards_of).reshape((-1,) + (1,) * (len(shape) - 1 - dim))
    return factor_of


def gaussian(rng, dims, scale, reach, cuts=(), kind=jnp.bfloat16):
    values = jax.random.normal(rng, dims, jnp.float32) * scale
    if len(cuts) > 0:
        values = block_scale(rng, dims, cuts, -0.22, 0.18) * values
    return jnp.clip(values, min=-reach, max=reach).astype(kind)


def setup_inputs(seed: int = 0) -> dict:
    seeds = jax.random.split(jax.random.key(seed), 14)
    state = draw_state(jax.random.fold_in(seeds[13], 71), 0)
    basis_projection_weight = gaussian(seeds[1], (FAC, BASIS), FAC ** -0.5, 0.5)
    factor_node_loading = gaussian(seeds[2], (FAC, NODES), 0.002, 0.011962891)
    curve = jnp.clip(jax.random.uniform(seeds[3], (NODES,), jnp.float32, 0.01, 0.05), 0.01, 0.05)
    discount = jnp.clip(0.7 + 0.3 * jax.random.uniform(seeds[4], (EXD, PATHS), jnp.float32) ** block_scale(seeds[4], (EXD, PATHS), ((1, 16),), -0.2, 0.2), 0.7, 1.0)
    region = set_ends(jax.random.randint(seeds[5], (EXD, PATHS, TRADE_GROUPS), 0, 3), jax.random.fold_in(seeds[5], 1), 0, 2).astype(jnp.int32)
    carry_in = draw_carry_in(jax.random.fold_in(seeds[13], 71), 0)
    group_of = draw_group_of(jax.random.fold_in(seeds[13], 71), 0)
    swap_start = set_ends(jax.random.randint(seeds[8], (TRADES,), 0, NODES // 2), jax.random.fold_in(seeds[8], 1), 0, (NODES // 2) - 1).astype(jnp.int32)
    swap_length = set_ends(jax.random.randint(seeds[9], (TRADES,), 8, NODES // 2), jax.random.fold_in(seeds[9], 1), 8, (NODES // 2) - 1).astype(jnp.int32)
    strike = jnp.clip(0.01 + 0.04 * jax.random.uniform(seeds[10], (TRADES,), jnp.float32) ** block_scale(seeds[10], (TRADES,), ((0, 8),), -0.2, 0.2), 0.01, 0.05)
    notional = gaussian(seeds[11], (TRADES,), 0.1, 0.6, ((0, 8),), jnp.float32)
    bucket_map = gaussian(seeds[12], (NODES, BUCKETS), NODES ** -0.5, 0.1875, (), jnp.float32)
    return {"state": state, "basis_projection_weight": basis_projection_weight, "factor_node_loading": factor_node_loading, "curve": curve, "discount": discount, "region": region, "carry_in": carry_in, "group_of": group_of, "swap_start": swap_start, "swap_length": swap_length, "strike": strike, "notional": notional, "bucket_map": bucket_map}


ridge_share = 0.05
horizon = 30.0

def node_grid():
    return horizon * (jnp.arange(NODES, dtype=jnp.float32) + 1.0) / NODES

def discount_curve(state_now, factor_node_loading, curve):
    shock = jnp.dot(state_now.astype(jnp.float32), factor_node_loading.astype(jnp.float32), preferred_element_type=jnp.float32)
    return jnp.exp(-node_grid()[None, :] * (curve[None, :] + shock))

def cash_matrix(swap_start, swap_length, strike, notional):
    nodes = jnp.arange(NODES, dtype=jnp.int32)[None, :]
    first = swap_start[:, None]
    final = first + swap_length[:, None]
    opening = (nodes == first).astype(jnp.float32)
    closing = (nodes == final).astype(jnp.float32)
    coupons = ((nodes > first) & (nodes <= final)).astype(jnp.float32)
    return notional[:, None] * (opening - closing - strike[:, None] * (horizon / NODES) * coupons)

def solve_groups(lower_factor, right_side_rows):
    column = right_side_rows[:, :, None]
    middle = lax.linalg.triangular_solve(lower_factor, column, left_side=True, lower=True)
    result = lax.linalg.triangular_solve(lower_factor, middle, left_side=True, lower=True, transpose_a=True)
    return result[:, :, 0]

def reference(state, basis_projection_weight, factor_node_loading, curve, discount, region, carry_in, group_of, swap_start, swap_length, strike, notional, bucket_map):
    members = (group_of[:, None] == jnp.arange(TRADE_GROUPS, dtype=jnp.int32)[None, :]).astype(jnp.float32)
    group_cash = jnp.dot(members.T, cash_matrix(swap_start, swap_length, strike, notional), precision=lax.Precision.HIGHEST)
    ridge_term = ridge_share * PATHS * jnp.eye(BASIS, dtype=jnp.float32)
    values = carry_in
    factor_list = [None] * EXD
    feature_list = [None] * EXD
    coefficient_list = [None] * EXD
    for moment_matrix in reversed(range(EXD)):
        node_df = discount_curve(state[moment_matrix], factor_node_loading, curve)
        payoff = jnp.dot(node_df, group_cash.T, precision=lax.Precision.HIGHEST)
        features = jnp.tanh(jnp.dot(state[moment_matrix].astype(jnp.float32), basis_projection_weight.astype(jnp.float32), preferred_element_type=jnp.float32)).astype(jnp.bfloat16)
        in_money = (region[moment_matrix] >= 1).astype(jnp.float32)
        holding = (region[moment_matrix] == 1).astype(jnp.float32)
        exercised = (region[moment_matrix] == 2).astype(jnp.float32)
        outside = (region[moment_matrix] == 0).astype(jnp.float32)
        target = discount[moment_matrix][:, None] * values
        grams = lax.map(lambda column: jnp.dot((features * column[:, None].astype(jnp.bfloat16)).T.astype(jnp.float32), features.astype(jnp.float32), preferred_element_type=jnp.float32), in_money.T)
        grams = grams + ridge_term[None]
        projection = jnp.dot(features.T.astype(jnp.float32), (in_money * target).astype(jnp.bfloat16).astype(jnp.float32), preferred_element_type=jnp.float32).T
        lower_factor = jnp.linalg.cholesky(grams)
        coefficient = solve_groups(lower_factor, projection)
        fitted = jnp.dot(features.astype(jnp.float32), coefficient.T.astype(jnp.bfloat16).astype(jnp.float32), preferred_element_type=jnp.float32)
        values = exercised * payoff + holding * fitted + outside * target
        factor_list[moment_matrix] = lower_factor
        feature_list[moment_matrix] = features
        coefficient_list[moment_matrix] = coefficient
    adjoint_value = jnp.full(values.shape, 1.0 / PATHS, dtype=jnp.float32)
    node_total = jnp.zeros((NODES,), jnp.float32)
    for moment_matrix in range(EXD):
        holding = (region[moment_matrix] == 1).astype(jnp.float32)
        exercised = (region[moment_matrix] == 2).astype(jnp.float32)
        outside = (region[moment_matrix] == 0).astype(jnp.float32)
        in_money = (region[moment_matrix] >= 1).astype(jnp.float32)
        weight = exercised * adjoint_value
        node_df = discount_curve(state[moment_matrix], factor_node_loading, curve)
        node_total = node_total + jnp.sum(group_cash * jnp.dot(weight.T, node_df, precision=lax.Precision.HIGHEST), axis=0)
        if moment_matrix < EXD - 1:
            features = feature_list[moment_matrix]
            pulled = jnp.dot(features.T.astype(jnp.float32), (holding * adjoint_value).astype(jnp.bfloat16).astype(jnp.float32), preferred_element_type=jnp.float32).T
            back = solve_groups(factor_list[moment_matrix], pulled)
            spread = jnp.dot(features.astype(jnp.float32), back.T.astype(jnp.bfloat16).astype(jnp.float32), preferred_element_type=jnp.float32)
            adjoint_value = discount[moment_matrix][:, None] * (outside * adjoint_value + in_money * spread)
    node_adjoint = -node_grid() * node_total
    bucketed = jnp.dot(node_adjoint[None, :], bucket_map, precision=lax.Precision.HIGHEST)[0]
    return (values, jnp.stack(coefficient_list), node_adjoint, bucketed)
```

```python
import jax
import jax.numpy as jnp
from jax import lax
from jax.experimental import pallas as pl
from jax.experimental.pallas import tpu as pltpu
from jax.sharding import Mesh
from jax.sharding import PartitionSpec as P

EXD = 3
BASIS = 256
NODES = 1024
FAC = 128
GRP = 4
LOCAL = 1024
TRADES = 2500
TPAD = 2560
PATHS = 16384
PATH = ("path_0", "path_1", "path_2")
TRADE = ("trade_0", "trade_1")
MESH = pl.DeviceIdType.MESH
HIGH = lax.Precision.HIGHEST
F32 = jnp.float32
BF16 = jnp.bfloat16
ROWS = 264

ridge_share = 0.05
horizon = 30.0
BOUND = (BASIS + ridge_share) * PATHS

NT = (((1,), (1,)), ((), ()))
NN = (((1,), (0,)), ((), ()))


def dot(a, b, dims=NN, precision=None):
    return lax.dot_general(a, b, dims, precision=precision, preferred_element_type=F32)


def split3(x):
    one = x.astype(BF16).astype(F32)
    rest = x - one
    two = rest.astype(BF16).astype(F32)
    return one, two, (rest - two).astype(BF16).astype(F32)


def stack3(x):
    pieces = split3(x)
    return jnp.concatenate([*pieces, jnp.zeros_like(x)], axis=0).astype(BF16)


def polynomials():
    low, high = ridge_share * PATHS / BOUND, 1.0
    steps = []
    while not steps or high - 1.0 > 2e-6:
        width, middle = high - low, high + low
        scale = 2.0 * (middle / width) ** 2 - 1.0
        steps.append((8.0 * middle / width**2 / scale, 8.0 / width**2 / scale))
        low, high = 1.0 - 1.0 / scale, 1.0 + 1.0 / scale
    return steps


def dot3(a, b):
    a_hi, b_hi = a.astype(BF16), b.astype(BF16)
    a_lo = (a - a_hi.astype(F32)).astype(BF16)
    b_lo = (b - b_hi.astype(F32)).astype(BF16)
    return dot(a_hi, b_hi) + (dot(a_hi, b_lo) + dot(a_lo, b_hi))


def invert(a):
    eye = (
        lax.broadcasted_iota(jnp.int32, (BASIS, BASIS), 0) == lax.broadcasted_iota(jnp.int32, (BASIS, BASIS), 1)
    ).astype(F32)
    a = a * (1.0 / BOUND)
    (alpha, beta), *others, last = polynomials()
    inverse = alpha * eye - beta * a
    product = dot3(a, inverse)
    for alpha, beta in others:
        both = dot3(jnp.concatenate([inverse, product], axis=0), alpha * eye - beta * product)
        inverse, product = both[:BASIS], both[BASIS:]
    alpha, beta = last
    product = dot(a, inverse, NN, HIGH)
    return dot(inverse, alpha * eye - beta * product, NN, HIGH) * (1.0 / BOUND)


def kernel(
    state,
    weight,
    loading,
    curve,
    discount,
    region,
    carry,
    group_of,
    swap_start,
    swap_length,
    strike,
    notional,
    bucket_map,
    values_out,
    coefficient_out,
    node_out,
    bucket_out,
    ft,
    rhs,
    away,
    home,
    got_core,
    got_z,
    got_y,
    df_hi,
    df_lo,
    ints,
    floats,
    payoff,
    inverse_ref,
    answer_src,
    answer_a,
    answer_b,
    answer_c,
    part_b,
    part_c,
    gather_b,
    gather_c,
    node_one,
    node_two,
    core_send,
    core_recv,
    z_send,
    z_recv,
    y_send,
    y_recv,
    a_send,
    a_recv,
    b_send,
    b_recv,
    bb_send,
    bb_recv,
    c_send,
    c_recv,
    cc_send,
    cc_recv,
    n1_send,
    n1_recv,
    n2_send,
    n2_recv,
):
    yh = lax.axis_index("path_0")
    z = lax.axis_index("path_1")
    core = lax.axis_index("path_2")
    yl = lax.axis_index("trade_0")
    x = lax.axis_index("trade_1")
    me = yh * 8 + z * 2 + core
    tme = yl * 4 + x
    mine = core * 2 + yh

    def path_id(p):
        return {"path_0": p // 8, "path_1": (p // 2) % 4, "path_2": p % 2}

    def trade_id(t):
        return {"trade_0": t // 4, "trade_1": t % 4}

    def remote(src, dst, send, recv, device):
        return pltpu.make_async_remote_copy(
            src_ref=src, dst_ref=dst, send_sem=send, recv_sem=recv, device_id=device, device_id_type=MESH
        )

    barrier = pltpu.get_barrier_semaphore()
    for k in range(1, 16):
        pl.semaphore_signal(barrier, inc=1, device_id=path_id((me + k) % 16), device_id_type=MESH)
    for k in range(1, 8):
        pl.semaphore_signal(barrier, inc=1, device_id=trade_id((tme + k) % 8), device_id_type=MESH)

    def features(i, _):
        chunk = state[pl.ds(pl.multiple_of(i * 256, 256), 256), :]
        wide = lax.dot_general(weight[...], chunk, (((0,), (1,)), ((), ())), preferred_element_type=F32)
        ft[i // 4, :, pl.ds(pl.multiple_of((i % 4) * 256, 256), 256)] = jnp.tanh(wide).astype(BF16)
        return 0

    lax.fori_loop(0, 12, features, 0)

    def masks(d):
        r = region[d]
        return (
            (r >= 1).astype(F32),
            (r == 1).astype(F32),
            (r == 2).astype(F32),
            (r == 0).astype(F32),
        )

    def project(rows8, d):
        return dot(rows8.astype(BF16), ft[d], NT)

    zero4 = jnp.zeros((4, LOCAL), F32)
    target2 = discount[2:3, :] * carry[...]
    rhs[2] = project(jnp.concatenate([masks(2)[0] * target2, zero4], axis=0), 2)
    rhs[1] = jnp.zeros((8, BASIS), F32)
    rhs[0] = project(jnp.concatenate([masks(0)[1] * (1.0 / PATHS), zero4], axis=0), 0)

    r128 = lax.broadcasted_iota(jnp.int32, (128, 128), 0)
    c128 = lax.broadcasted_iota(jnp.int32, (128, 128), 1)

    def gram(d, g, out, slot):
        mask = jnp.where(region[d, pl.ds(g, 1), :] >= 1, 1.0, 0.0).astype(BF16)
        f = ft[d]
        masked = f * mask
        top = dot(masked[0:128], f[0:128], NT)
        low = dot(masked[128:256], f, NT)
        last = low[:, 128:256]
        out[slot, 0:128, :] = jnp.where(r128 >= c128, top, last)
        out[slot, 128:256, :] = low[:, 0:128]
        diagonal = jnp.sum(jnp.where(r128 == c128, last, 0.0), axis=0, keepdims=True)
        right = rhs[d, pl.ds(g, 1), :]
        out[slot, 256:264, :] = jnp.concatenate(
            [diagonal, right[:, 0:128], right[:, 128:256], jnp.zeros((5, 128), F32)], axis=0
        )

    pl.semaphore_wait(barrier, 22)

    def core_copy(i):
        return remote(away.at[i], got_core.at[i], core_send.at[i], core_recv.at[i], {"path_2": 1 - core})

    def send_away(i, _):
        gram(i // 2, (1 - core) * 2 + i % 2, away, i)
        core_copy(i).start()
        return 0

    lax.fori_loop(0, 6, send_away, 0)

    def keep_home(i, _):
        gram(i // 2, core * 2 + i % 2, home, i)
        return 0

    lax.fori_loop(0, 6, keep_home, 0)

    def z_copy(i, d):
        slot = (z - d + 3) % 4
        at = slot * 2 + i % 2
        return remote(home.at[i], got_z.at[at], z_send.at[i], z_recv.at[at], {"path_1": d})

    def send_z(i, _):
        d = i // 2
        core_copy(i).wait()
        home[i] = home[i] + got_core[i]

        @pl.when(z != d)
        def _():
            z_copy(i, d).start()

        return 0

    lax.fori_loop(0, 6, send_z, 0)

    ints[...] = jnp.zeros_like(ints)
    floats[...] = jnp.zeros_like(floats)
    starts, amounts = swap_start[...].reshape(1, TRADES), notional[...].reshape(1, TRADES)
    ints[0:1, 0:TRADES] = group_of[...].reshape(1, TRADES) - tme * GRP
    ints[1:2, 0:TRADES] = starts
    ints[2:3, 0:TRADES] = starts + swap_length[...].reshape(1, TRADES)
    floats[0:1, 0:TRADES] = amounts
    floats[1:2, 0:TRADES] = amounts * (strike[...].reshape(1, TRADES) * (horizon / NODES))
    i32 = lax.broadcasted_iota(jnp.int32, (32, 512), 0)
    i128 = lax.broadcasted_iota(jnp.int32, (128, 512), 0)

    def histogram(i, total):
        span = pl.ds(pl.multiple_of(i * 512, 512), 512)
        group = ints[0:1, span]
        pieces = [*split3(floats[0:1, span]), *split3(floats[1:2, span])]
        for row, sign in ((1, 1.0), (2, -1.0)):
            key = ints[row : row + 1, span]
            hit = i32 == (key // 128) * 4 + group
            left = jnp.concatenate([jnp.where(hit, sign * piece, 0.0) for piece in pieces], axis=0).astype(BF16)
            right = (i128 == key % 128).astype(F32).astype(BF16)
            total = total + dot(left, right, NT)
        return total

    table = lax.fori_loop(0, 5, histogram, jnp.zeros((192, 128), F32))
    steps = table[0:32] + table[32:64] + table[64:96]
    slopes = table[96:128] + table[128:160] + table[160:192]
    before = (r128 < c128).astype(F32)
    ra = lax.broadcasted_iota(jnp.int32, (32, 32), 0)
    ca = lax.broadcasted_iota(jnp.int32, (32, 32), 1)
    earlier = ((ca // 4 < ra // 4) & (ca % 4 == ra % 4)).astype(F32)
    coupon = dot(slopes, before, NN, HIGH) + jnp.sum(dot(earlier, slopes, NN, HIGH), axis=1, keepdims=True)
    flat = steps - coupon
    cash = jnp.concatenate([flat[4 * a : 4 * a + 4, :] for a in range(8)], axis=1)
    cash_stack = stack3(cash)

    times = (lax.broadcasted_iota(jnp.int32, (1, NODES), 1).astype(F32) + 1.0) * (horizon / NODES)
    curve_row = curve[...]

    def sum3(t):
        return t[0:4] + t[4:8] + t[8:12]

    def discounting(i, _):
        span = pl.ds(pl.multiple_of(i * 256, 256), 256)
        shock = dot(state[span, :], loading[...])
        factor = jnp.exp(-times * (curve_row + shock))
        hi = factor.astype(BF16)
        lo = (factor - hi.astype(F32)).astype(BF16)
        df_hi[span, :] = hi
        df_lo[span, :] = lo
        payoff[i] = sum3(dot(cash_stack, hi, NT) + dot(cash_stack, lo, NT))
        return 0

    lax.fori_loop(0, 12, discounting, 0)

    def node_sum(w, d):
        stack = stack3(w)
        span = pl.ds(d * LOCAL, LOCAL)
        t = sum3(dot(stack, df_hi[span, :]) + dot(stack, df_lo[span, :]))
        return jnp.sum(cash * t, axis=0, keepdims=True)

    @pl.when(z < 3)
    def _():
        for j in range(2):
            total = home[z * 2 + j]
            for slot in range(3):
                z_copy_wait = remote(
                    home.at[0], got_z.at[slot * 2 + j], z_send.at[0], z_recv.at[slot * 2 + j], {"path_1": 0}
                )
                z_copy_wait.wait_recv()
                total = total + got_z[slot * 2 + j]
            home[z * 2 + j] = total

    def y_copy():
        return remote(home.at[z * 2 + 1 - yh], got_y, y_send, y_recv, {"path_0": 1 - yh})

    @pl.when(z < 3)
    def _():
        y_copy().start()

    in0, hold0, ex0, out0 = masks(0)
    bar0 = jnp.full((4, LOCAL), 1.0 / PATHS, F32)
    node_total = node_sum(ex0 * bar0, 0)

    def solve(rows8):
        return dot(rows8, inverse_ref[...], NN, HIGH)

    def broadcast(dst, sends, recvs, at):
        def go(k, _):
            remote(answer_src, dst.at[at], sends.at[k - 1], recvs.at[at], path_id((me + k) % 16)).start()
            return 0

        lax.fori_loop(1, 16, go, 0)

    def broadcast_done(dst, sends, recvs, at):
        def go(k, _):
            remote(answer_src, dst.at[at], sends.at[k - 1], recvs.at[at], path_id((me + k) % 16)).wait_send()
            return 0

        lax.fori_loop(1, 16, go, 0)

    def collect(dst, sends, recvs, at, owner):
        @pl.when(me != owner)
        def _():
            remote(answer_src, dst.at[at], sends.at[0], recvs.at[at], path_id(owner)).wait_recv()

    def owner_of(d, g):
        return (g % 2) * 8 + d * 2 + g // 2

    @pl.when(z < 3)
    def _():
        y_copy().wait()
        packed = home[z * 2 + yh] + got_y[...]
        mix = packed[0:128]
        flip = mix.T
        b = packed[128:256]
        ridge = jnp.where(r128 == c128, ridge_share * PATHS, 0.0)
        a = jnp.where(r128 >= c128, mix, flip) + ridge
        c = jnp.where(r128 < c128, mix, jnp.where(r128 > c128, flip, packed[256:257])) + ridge
        full = jnp.concatenate(
            [jnp.concatenate([a, b.T], axis=1), jnp.concatenate([b, c], axis=1)], axis=0
        )
        inverse_ref[...] = invert(full)

        @pl.when(z != 1)
        def _():
            at = (1 - z // 2) * 4 + mine
            row = jnp.concatenate([packed[257:258], packed[258:259]], axis=1)
            answer = solve(jnp.broadcast_to(row, (8, BASIS)))
            answer_src[...] = answer
            answer_a[at] = answer
            broadcast(answer_a, a_send, a_recv, at)

    for g in range(4):
        collect(answer_a, a_send, a_recv, g, owner_of(2, g))
        collect(answer_a, a_send, a_recv, 4 + g, owner_of(0, g))

    def pick(buffer, base, row):
        return jnp.concatenate(
            [buffer[base + g, row + (g if row >= 0 else 1) : row + (g if row >= 0 else 1) + 1, :] for g in range(4)],
            axis=0,
        )

    def payoff_of(d):
        return jnp.concatenate([payoff[4 * d + k] for k in range(4)], axis=1)

    def fit(coefficient, d):
        stacked = jnp.concatenate([coefficient, jnp.zeros_like(coefficient)], axis=0).astype(BF16)
        return dot(stacked, ft[d])[0:4]

    coef2 = pick(answer_a, 0, -1)
    back0 = pick(answer_a, 4, -1)
    coefficient_out[2] = coef2
    in1, hold1, ex1, out1 = masks(1)
    in2, hold2, ex2, out2 = masks(2)
    values2 = ex2 * payoff_of(2) + hold2 * fit(coef2, 2) + out2 * target2
    bar1 = discount[0:1, :] * (out0 * bar0 + in0 * fit(back0, 0))
    target1 = discount[1:2, :] * values2
    part_b[...] = project(jnp.concatenate([in1 * target1, hold1 * bar1], axis=0), 1)
    gather_b[me] = part_b[...]

    def gather(src, dst, sends, recvs, d):
        for g in range(4):
            owner = owner_of(d, g)

            @pl.when(me != owner)
            def _():
                remote(src, dst.at[me], sends.at[g], recvs.at[me], path_id(owner)).start()

    def gather_sent(src, dst, sends, recvs, d):
        for g in range(4):
            owner = owner_of(d, g)

            @pl.when(me != owner)
            def _():
                remote(src, dst.at[me], sends.at[g], recvs.at[me], path_id(owner)).wait_send()

    def gathered(src, dst, sends, recvs):
        def go(k, _):
            p = (me + k) % 16
            remote(src, dst.at[p], sends.at[0], recvs.at[p], path_id(p)).wait_recv()
            return 0

        lax.fori_loop(1, 16, go, 0)
        total = dst[0]
        for p in range(1, 16):
            total = total + dst[p]
        return total

    gather(part_b, gather_b, b_send, b_recv, 1)
    node_total = node_total + node_sum(ex1 * bar1, 1)

    @pl.when(z == 1)
    def _():
        answer = solve(gathered(part_b, gather_b, b_send, b_recv))
        answer_src[...] = answer
        answer_b[mine] = answer
        broadcast(answer_b, bb_send, bb_recv, mine)

    for g in range(4):
        collect(answer_b, bb_send, bb_recv, g, owner_of(1, g))
    coef1 = pick(answer_b, 0, 0)
    back1 = pick(answer_b, 0, 4)
    coefficient_out[1] = coef1
    values1 = ex1 * payoff_of(1) + hold1 * fit(coef1, 1) + out1 * target1
    target0 = discount[0:1, :] * values1
    part_c[...] = project(jnp.concatenate([in0 * target0, zero4], axis=0), 0)
    gather_c[me] = part_c[...]
    gather(part_c, gather_c, c_send, c_recv, 0)

    @pl.when(z == 0)
    def _():
        answer = solve(gathered(part_c, gather_c, c_send, c_recv))
        broadcast_done(answer_a, a_send, a_recv, 4 + mine)
        answer_src[...] = answer
        answer_c[mine] = answer
        broadcast(answer_c, cc_send, cc_recv, mine)

    bar2 = discount[1:2, :] * (out1 * bar1 + in1 * fit(back1, 1))
    node_total = node_total + node_sum(ex2 * bar2, 2)
    tile = jnp.concatenate([node_total[:, 128 * k : 128 * k + 128] for k in range(8)], axis=0)
    node_one[me] = tile

    def one_copy(k):
        return remote(
            node_one.at[me], node_one.at[me], n1_send.at[k - 1], n1_recv.at[me], path_id((me + k) % 16)
        )

    def one_arrival(k):
        p = (me + k) % 16
        return remote(node_one.at[me], node_one.at[p], n1_send.at[0], n1_recv.at[p], path_id(p))

    def two_copy(k):
        return remote(
            node_two.at[tme], node_two.at[tme], n2_send.at[k - 1], n2_recv.at[tme], trade_id((tme + k) % 8)
        )

    def two_arrival(k):
        t = (tme + k) % 8
        return remote(node_two.at[tme], node_two.at[t], n2_send.at[0], n2_recv.at[t], trade_id(t))

    def run(first, last, f):
        def go(k, _):
            f(k)
            return 0

        lax.fori_loop(first, last, go, 0)

    run(1, 16, lambda k: one_copy(k).start())
    run(1, 16, lambda k: one_arrival(k).wait_recv())
    total = node_one[0]
    for p in range(1, 16):
        total = total + node_one[p]
    node_two[tme] = total
    run(1, 8, lambda k: two_copy(k).start())

    for g in range(4):
        collect(answer_c, cc_send, cc_recv, g, owner_of(0, g))
    coef0 = pick(answer_c, 0, 0)
    coefficient_out[0] = coef0
    values_out[...] = ex0 * payoff_of(0) + hold0 * fit(coef0, 0) + out0 * target0

    run(1, 8, lambda k: two_arrival(k).wait_recv())
    total = node_two[0]
    for t in range(1, 8):
        total = total + node_two[t]
    grid = (
        lax.broadcasted_iota(jnp.int32, (8, 128), 0) * 128 + lax.broadcasted_iota(jnp.int32, (8, 128), 1)
    ).astype(F32)
    adjoint = -((grid + 1.0) * (horizon / NODES)) * total
    node_out[...] = adjoint
    line = jnp.concatenate([adjoint[k : k + 1, :] for k in range(8)], axis=1)
    bucket_out[...] = dot(jnp.broadcast_to(line, (8, NODES)), bucket_map[...], NT, HIGH)

    def z_sent(i, _):
        d = i // 2

        @pl.when(z != d)
        def _():
            z_copy(i, d).wait_send()

        return 0

    lax.fori_loop(0, 6, z_sent, 0)
    gather_sent(part_b, gather_b, b_send, b_recv, 1)
    gather_sent(part_c, gather_c, c_send, c_recv, 0)

    @pl.when(z == 2)
    def _():
        broadcast_done(answer_a, a_send, a_recv, mine)

    @pl.when(z == 1)
    def _():
        broadcast_done(answer_b, bb_send, bb_recv, mine)

    @pl.when(z == 0)
    def _():
        broadcast_done(answer_c, cc_send, cc_recv, mine)

    run(1, 16, lambda k: one_copy(k).wait_send())
    run(1, 8, lambda k: two_copy(k).wait_send())


def finish(values, coefficients, node, bucketed, values_out, coefficients_out, node_out, bucketed_out):
    values_out[...] = values[...]
    coefficients_out[...] = coefficients[...]
    node_out[...] = node[...].reshape(NODES)
    bucketed_out[...] = bucketed[0:1, :].reshape(64)


def shards(
    state,
    basis_projection_weight,
    factor_node_loading,
    curve,
    discount,
    region,
    carry_in,
    group_of,
    swap_start,
    swap_length,
    strike,
    notional,
    bucket_map,
):
    vmem = pl.BlockSpec(memory_space=pltpu.VMEM)
    dma = pltpu.SemaphoreType.DMA
    values, coefficients, node, bucketed = pl.pallas_call(
        kernel,
        out_shape=(
            jax.ShapeDtypeStruct((GRP, LOCAL), F32),
            jax.ShapeDtypeStruct((EXD, GRP, BASIS), F32),
            jax.ShapeDtypeStruct((8, 128), F32),
            jax.ShapeDtypeStruct((8, 64), F32),
        ),
        in_specs=[vmem] * 13,
        out_specs=(vmem,) * 4,
        scratch_shapes=[
            pltpu.VMEM((EXD, BASIS, LOCAL), BF16),
            pltpu.VMEM((EXD, 8, BASIS), F32),
            pltpu.VMEM((6, ROWS, 128), F32),
            pltpu.VMEM((6, ROWS, 128), F32),
            pltpu.VMEM((6, ROWS, 128), F32),
            pltpu.VMEM((6, ROWS, 128), F32),
            pltpu.VMEM((ROWS, 128), F32),
            pltpu.VMEM((EXD * LOCAL, NODES), BF16),
            pltpu.VMEM((EXD * LOCAL, NODES), BF16),
            pltpu.VMEM((8, TPAD), jnp.int32),
            pltpu.VMEM((8, TPAD), F32),
            pltpu.VMEM((12, GRP, 256), F32),
            pltpu.VMEM((BASIS, BASIS), F32),
            pltpu.VMEM((8, BASIS), F32),
            pltpu.VMEM((8, 8, BASIS), F32),
            pltpu.VMEM((4, 8, BASIS), F32),
            pltpu.VMEM((4, 8, BASIS), F32),
            pltpu.VMEM((8, BASIS), F32),
            pltpu.VMEM((8, BASIS), F32),
            pltpu.VMEM((16, 8, BASIS), F32),
            pltpu.VMEM((16, 8, BASIS), F32),
            pltpu.VMEM((16, 8, 128), F32),
            pltpu.VMEM((8, 8, 128), F32),
            dma((6,)),
            dma((6,)),
            dma((6,)),
            dma((6,)),
            dma,
            dma,
            dma((15,)),
            dma((8,)),
            dma((4,)),
            dma((16,)),
            dma((15,)),
            dma((4,)),
            dma((4,)),
            dma((16,)),
            dma((15,)),
            dma((4,)),
            dma((15,)),
            dma((16,)),
            dma((7,)),
            dma((8,)),
        ],
        compiler_params=pltpu.CompilerParams(collective_id=0, has_side_effects=True),
        name="backward_window",
    )(
        state.reshape(EXD * LOCAL, FAC),
        basis_projection_weight,
        factor_node_loading,
        curve.reshape(1, NODES),
        discount,
        region.transpose(0, 2, 1),
        carry_in.T,
        group_of,
        swap_start,
        swap_length,
        strike,
        notional,
        bucket_map.T,
    )
    values, coefficients, node, bucketed = pl.pallas_call(
        finish,
        out_shape=(
            jax.ShapeDtypeStruct((GRP, LOCAL), F32),
            jax.ShapeDtypeStruct((EXD, GRP, BASIS), F32),
            jax.ShapeDtypeStruct((NODES,), F32),
            jax.ShapeDtypeStruct((64,), F32),
        ),
        in_specs=[vmem] * 4,
        out_specs=(vmem,) * 4,
        name="finish",
    )(values, coefficients, node, bucketed)
    return (values.T, coefficients, node, bucketed)


def solution(mesh):
    torus = Mesh(
        mesh.devices.reshape(2, 4, 2, 2, 4), ("path_0", "path_1", "path_2", "trade_0", "trade_1")
    )
    in_specs = (
        P(None, PATH, None),
        P(),
        P(),
        P(),
        P(None, PATH),
        P(None, PATH, TRADE),
        P(PATH, TRADE),
        P(TRADE),
        P(TRADE),
        P(TRADE),
        P(TRADE),
        P(TRADE),
        P(),
    )
    out_specs = (P(PATH, TRADE), P(None, TRADE, None), P(), P())
    return jax.shard_map(
        shards, mesh=torus, in_specs=in_specs, out_specs=out_specs, check_vma=False
    )
```

```python
import jax
import jax.numpy as jnp
from jax import lax
from jax.experimental import pallas as pl
from jax.experimental.pallas import tpu as pltpu
from jax.sharding import Mesh
from jax.sharding import PartitionSpec as P

EXD = 3
BASIS = 256
NODES = 1024
FAC = 128
GRP = 4
LOCAL = 1024
TRADES = 2500
TPAD = 2560
PATHS = 16384
PATH = ("path_0", "path_1", "path_2")
TRADE = ("trade_0", "trade_1")
MESH = pl.DeviceIdType.MESH
HIGH = lax.Precision.HIGHEST
F32 = jnp.float32
BF16 = jnp.bfloat16
ROWS = 264
DATES = (2, 0, 1)

ridge_share = 0.05
horizon = 30.0
BOUND = (BASIS + ridge_share) * PATHS

NT = (((1,), (1,)), ((), ()))
NN = (((1,), (0,)), ((), ()))


def dot(a, b, dims=NN, precision=None):
    return lax.dot_general(a, b, dims, precision=precision, preferred_element_type=F32)


def split3(x):
    one = x.astype(BF16).astype(F32)
    rest = x - one
    two = rest.astype(BF16).astype(F32)
    return one, two, (rest - two).astype(BF16).astype(F32)


def stack3(x):
    pieces = split3(x)
    return jnp.concatenate([*pieces, jnp.zeros_like(x)], axis=0).astype(BF16)


def polynomials():
    low, high = ridge_share * PATHS / BOUND, 1.0
    steps = []
    while not steps or high - 1.0 > 2e-6:
        width, middle = high - low, high + low
        scale = 2.0 * (middle / width) ** 2 - 1.0
        steps.append((8.0 * middle / width**2 / scale, 8.0 / width**2 / scale))
        low, high = 1.0 - 1.0 / scale, 1.0 + 1.0 / scale
    return steps


def dot3(a, b):
    a_hi, b_hi = a.astype(BF16), b.astype(BF16)
    a_lo = (a - a_hi.astype(F32)).astype(BF16)
    b_lo = (b - b_hi.astype(F32)).astype(BF16)
    return dot(a_hi, b_hi) + (dot(a_hi, b_lo) + dot(a_lo, b_hi))


def invert(a):
    eye = (
        lax.broadcasted_iota(jnp.int32, (BASIS, BASIS), 0) == lax.broadcasted_iota(jnp.int32, (BASIS, BASIS), 1)
    ).astype(F32)
    a = a * (1.0 / BOUND)
    (alpha, beta), *others, last = polynomials()
    inverse = alpha * eye - beta * a
    product = dot3(a, inverse)
    for alpha, beta in others:
        both = dot3(jnp.concatenate([inverse, product], axis=0), alpha * eye - beta * product)
        inverse, product = both[:BASIS], both[BASIS:]
    alpha, beta = last
    product = dot(a, inverse, NN, HIGH)
    return dot(inverse, alpha * eye - beta * product, NN, HIGH) * (1.0 / BOUND)


def kernel(
    state,
    weight,
    loading,
    curve,
    discount,
    region,
    carry,
    group_of,
    swap_start,
    swap_length,
    strike,
    notional,
    bucket_map,
    values_out,
    coefficient_out,
    node_out,
    bucket_out,
    ft,
    rhs,
    away,
    home,
    got_core,
    got,
    df_hi,
    df_lo,
    ints,
    floats,
    payoff,
    inverse_ref,
    answer_src,
    answer_a,
    answer_b,
    answer_c,
    part_b,
    part_c,
    gather_b,
    gather_c,
    node_one,
    node_two,
    core_send,
    core_recv,
    owner_send,
    owner_recv,
    a_send,
    a_recv,
    b_send,
    b_recv,
    bb_send,
    bb_recv,
    c_send,
    c_recv,
    cc_send,
    cc_recv,
    n1_send,
    n1_recv,
    n2_send,
    n2_recv,
):
    yh = lax.axis_index("path_0")
    z = lax.axis_index("path_1")
    core = lax.axis_index("path_2")
    yl = lax.axis_index("trade_0")
    x = lax.axis_index("trade_1")
    me = yh * 8 + z * 2 + core
    tme = yl * 4 + x
    mine = core * 2 + yh

    def path_id(p):
        return {"path_0": p // 8, "path_1": (p // 2) % 4, "path_2": p % 2}

    def trade_id(t):
        return {"trade_0": t // 4, "trade_1": t % 4}

    def remote(src, dst, send, recv, device):
        return pltpu.make_async_remote_copy(
            src_ref=src, dst_ref=dst, send_sem=send, recv_sem=recv, device_id=device, device_id_type=MESH
        )

    barrier = pltpu.get_barrier_semaphore()
    for k in range(1, 16):
        pl.semaphore_signal(barrier, inc=1, device_id=path_id((me + k) % 16), device_id_type=MESH)
    for k in range(1, 8):
        pl.semaphore_signal(barrier, inc=1, device_id=trade_id((tme + k) % 8), device_id_type=MESH)

    weight_t = weight[...].T

    def features(d):
        for c in range(4):
            chunk = state[d * LOCAL + c * 256 : d * LOCAL + c * 256 + 256, :]
            ft[d, :, c * 256 : c * 256 + 256] = jnp.tanh(dot(weight_t, chunk, NT)).astype(BF16)

    def masks(d):
        r = region[d]
        return (
            (r >= 1).astype(F32),
            (r == 1).astype(F32),
            (r == 2).astype(F32),
            (r == 0).astype(F32),
        )

    def project(rows8, d):
        return dot(rows8.astype(BF16), ft[d], NT)

    zero4 = jnp.zeros((4, LOCAL), F32)
    bar0 = jnp.full((4, LOCAL), 1.0 / PATHS, F32)
    target2 = discount[2:3, :] * carry[...]
    in0, hold0, ex0, out0 = masks(0)
    in1, hold1, ex1, out1 = masks(1)
    in2, hold2, ex2, out2 = masks(2)

    r128 = lax.broadcasted_iota(jnp.int32, (128, 128), 0)
    c128 = lax.broadcasted_iota(jnp.int32, (128, 128), 1)

    def pack(out, slot, top, low, right):
        last = low[:, 128:256]
        out[slot, 0:128, :] = jnp.where(r128 >= c128, top, last)
        out[slot, 128:256, :] = low[:, 0:128]
        diagonal = jnp.sum(jnp.where(r128 == c128, last, 0.0), axis=0, keepdims=True)
        out[slot, 256:264, :] = jnp.concatenate(
            [diagonal, right[:, 0:128], right[:, 128:256], jnp.zeros((5, 128), F32)], axis=0
        )

    def grams(slot):
        d = DATES[slot // 2]
        j = yh if slot % 2 else 1 - yh
        f = ft[d]
        theirs = (1 - core) * 2 + j
        ours = core * 2 + j
        one = f * jnp.where(region[d, pl.ds(theirs, 1), :] >= 1, 1.0, 0.0).astype(BF16)
        two = f * jnp.where(region[d, pl.ds(ours, 1), :] >= 1, 1.0, 0.0).astype(BF16)
        top = dot(jnp.concatenate([one[0:128], two[0:128]], axis=0), f[0:128], NT)
        low = dot(jnp.concatenate([one[128:256], two[128:256]], axis=0), f, NT)
        pack(away, slot, top[0:128], low[0:128], rhs[d, pl.ds(theirs, 1), :])
        pack(home, slot, top[128:256], low[128:256], rhs[d, pl.ds(ours, 1), :])

    def core_copy(i):
        return remote(away.at[i], got_core.at[i], core_send.at[i], core_recv.at[i], {"path_2": 1 - core})

    def owner_copy(i):
        d, other = DATES[i // 2], 1 - i % 2
        at = 4 * other + (z - d + 4) % 4
        to = {"path_0": 1 - yh if other else yh, "path_1": d}
        return remote(home.at[i], got.at[at], owner_send.at[i], owner_recv.at[at], to)

    def combine(i):
        core_copy(i).wait()
        home[i] = home[i] + got_core[i]
        if i % 2:

            @pl.when(z != DATES[i // 2])
            def _():
                owner_copy(i).start()
        else:
            owner_copy(i).start()

    rhs[1] = jnp.zeros((8, BASIS), F32)
    features(2)
    rhs[2] = project(jnp.concatenate([in2 * target2, zero4], axis=0), 2)
    grams(0)
    grams(1)
    features(0)
    rhs[0] = project(jnp.concatenate([hold0 * bar0, zero4], axis=0), 0)
    grams(2)
    grams(3)
    pl.semaphore_wait(barrier, 22)
    for i in range(4):
        core_copy(i).start()
    features(1)
    grams(4)
    core_copy(4).start()
    for i in range(4):
        combine(i)
    grams(5)
    core_copy(5).start()

    ints[...] = jnp.zeros_like(ints)
    floats[...] = jnp.zeros_like(floats)
    starts, amounts = swap_start[...].reshape(1, TRADES), notional[...].reshape(1, TRADES)
    ints[0:1, 0:TRADES] = group_of[...].reshape(1, TRADES) - tme * GRP
    ints[1:2, 0:TRADES] = starts
    ints[2:3, 0:TRADES] = starts + swap_length[...].reshape(1, TRADES)
    floats[0:1, 0:TRADES] = amounts
    floats[1:2, 0:TRADES] = amounts * (strike[...].reshape(1, TRADES) * (horizon / NODES))
    i32 = lax.broadcasted_iota(jnp.int32, (32, 512), 0)
    i128 = lax.broadcasted_iota(jnp.int32, (128, 512), 0)

    def histogram(i, total):
        span = pl.ds(pl.multiple_of(i * 512, 512), 512)
        group = ints[0:1, span]
        pieces = [*split3(floats[0:1, span]), *split3(floats[1:2, span])]
        for row, sign in ((1, 1.0), (2, -1.0)):
            key = ints[row : row + 1, span]
            hit = i32 == (key // 128) * 4 + group
            left = jnp.concatenate([jnp.where(hit, sign * piece, 0.0) for piece in pieces], axis=0).astype(BF16)
            right = (i128 == key % 128).astype(F32).astype(BF16)
            total = total + dot(left, right, NT)
        return total

    table = lax.fori_loop(0, 5, histogram, jnp.zeros((192, 128), F32))
    steps = table[0:32] + table[32:64] + table[64:96]
    slopes = table[96:128] + table[128:160] + table[160:192]
    before = (r128 < c128).astype(F32)
    ra = lax.broadcasted_iota(jnp.int32, (32, 32), 0)
    ca = lax.broadcasted_iota(jnp.int32, (32, 32), 1)
    earlier = ((ca // 4 < ra // 4) & (ca % 4 == ra % 4)).astype(F32)
    coupon = dot(slopes, before, NN, HIGH) + jnp.sum(dot(earlier, slopes, NN, HIGH), axis=1, keepdims=True)
    flat = steps - coupon
    cash = jnp.concatenate([flat[4 * a : 4 * a + 4, :] for a in range(8)], axis=1)
    cash_stack = stack3(cash)

    times = (lax.broadcasted_iota(jnp.int32, (1, NODES), 1).astype(F32) + 1.0) * (horizon / NODES)
    curve_row = curve[...]

    def sum3(t):
        return t[0:4] + t[4:8] + t[8:12]

    def discounting(d):
        def chunk(i, _):
            span = pl.ds(pl.multiple_of(i * 256, 256), 256)
            shock = dot(state[span, :], loading[...])
            factor = jnp.exp(-times * (curve_row + shock))
            hi = factor.astype(BF16)
            lo = (factor - hi.astype(F32)).astype(BF16)
            df_hi[span, :] = hi
            df_lo[span, :] = lo
            payoff[i] = sum3(dot(cash_stack, hi, NT) + dot(cash_stack, lo, NT))
            return 0

        lax.fori_loop(4 * d, 4 * d + 4, chunk, 0)

    combine(4)
    combine(5)

    def node_sum(w, d):
        stack = stack3(w)
        span = pl.ds(d * LOCAL, LOCAL)
        t = sum3(dot(stack, df_hi[span, :]) + dot(stack, df_lo[span, :]))
        return jnp.sum(cash * t, axis=0, keepdims=True)

    discounting(2)

    discounting(0)

    def solve(rows):
        return dot(rows, inverse_ref[...], NN, HIGH)

    def run(first, last, f):
        def go(k, _):
            f(k)
            return 0

        lax.fori_loop(first, last, go, 0)

    def answer_copy(k, dst, sends, recvs, at):
        return remote(answer_src, dst.at[at], sends.at[k - 1], recvs.at[at], path_id((me + k) % 16))

    def broadcast(dst, sends, recvs, at):
        run(1, 16, lambda k: answer_copy(k, dst, sends, recvs, at).start())

    def broadcast_done(dst, sends, recvs, at):
        run(1, 16, lambda k: answer_copy(k, dst, sends, recvs, at).wait_send())

    def collect(dst, sends, recvs, at, owner):
        @pl.when(me != owner)
        def _():
            remote(answer_src, dst.at[at], sends.at[0], recvs.at[at], path_id(owner)).wait_recv()

    def owner_of(d, g):
        return (g % 2) * 8 + d * 2 + g // 2

    @pl.when(z < 3)
    def _():
        packed = home[2 * ((z + 1) % 3) + 1]
        for at in range(1, 8):
            remote(home.at[0], got.at[at], owner_send.at[0], owner_recv.at[at], {"path_1": 0}).wait_recv()
            packed = packed + got[at]
        mix = packed[0:128]
        flip = mix.T
        b = packed[128:256]
        ridge = jnp.where(r128 == c128, ridge_share * PATHS, 0.0)
        a = jnp.where(r128 >= c128, mix, flip) + ridge
        c = jnp.where(r128 < c128, mix, jnp.where(r128 > c128, flip, packed[256:257])) + ridge
        full = jnp.concatenate(
            [jnp.concatenate([a, b.T], axis=1), jnp.concatenate([b, c], axis=1)], axis=0
        )
        inverse_ref[...] = invert(full)

        @pl.when(z != 1)
        def _():
            at = (1 - z // 2) * 4 + mine
            row = jnp.concatenate([packed[257:258], packed[258:259]], axis=1)
            answer = solve(jnp.broadcast_to(row, (2, BASIS)))
            answer_src[...] = answer
            answer_a[at] = answer
            broadcast(answer_a, a_send, a_recv, at)

    node_total = node_sum(ex0 * bar0, 0)
    discounting(1)

    for g in range(4):
        collect(answer_a, a_send, a_recv, g, owner_of(2, g))
        collect(answer_a, a_send, a_recv, 4 + g, owner_of(0, g))

    def pick(buffer, base, row):
        return jnp.concatenate([buffer[base + g, row : row + 1, :] for g in range(4)], axis=0)

    def payoff_of(d):
        return jnp.concatenate([payoff[4 * d + k] for k in range(4)], axis=1)

    def fit(coefficient, d):
        stacked = jnp.concatenate([coefficient, jnp.zeros_like(coefficient)], axis=0).astype(BF16)
        return dot(stacked, ft[d])[0:4]

    coef2 = pick(answer_a, 0, 0)
    back0 = pick(answer_a, 4, 0)
    coefficient_out[2] = coef2
    values2 = ex2 * payoff_of(2) + hold2 * fit(coef2, 2) + out2 * target2
    bar1 = discount[0:1, :] * (out0 * bar0 + in0 * fit(back0, 0))
    target1 = discount[1:2, :] * values2

    def gather_copy(src, dst, sends, recvs, d, g):
        return remote(src.at[g], dst.at[me], sends.at[g], recvs.at[me], path_id(owner_of(d, g)))

    def gather(src, dst, sends, recvs, d, rows8):
        for g in range(4):
            src[g] = jnp.concatenate([rows8[g : g + 1], rows8[4 + g : 5 + g]], axis=0)
        for g in range(4):

            @pl.when(me != owner_of(d, g))
            def _():
                gather_copy(src, dst, sends, recvs, d, g).start()

        @pl.when(z == d)
        def _():
            dst[me] = src[mine]

    def gather_sent(src, dst, sends, recvs, d):
        for g in range(4):

            @pl.when(me != owner_of(d, g))
            def _():
                gather_copy(src, dst, sends, recvs, d, g).wait_send()

    def gathered(src, dst, sends, recvs):
        def arrival(k):
            p = (me + k) % 16
            remote(src.at[0], dst.at[p], sends.at[0], recvs.at[p], path_id(p)).wait_recv()

        run(1, 16, arrival)
        total = dst[0]
        for p in range(1, 16):
            total = total + dst[p]
        return total

    gather(
        part_b, gather_b, b_send, b_recv, 1, project(jnp.concatenate([in1 * target1, hold1 * bar1], axis=0), 1)
    )
    node_total = node_total + node_sum(ex1 * bar1, 1)

    @pl.when(z == 1)
    def _():
        answer = solve(gathered(part_b, gather_b, b_send, b_recv))
        answer_src[...] = answer
        answer_b[mine] = answer
        broadcast(answer_b, bb_send, bb_recv, mine)

    for g in range(4):
        collect(answer_b, bb_send, bb_recv, g, owner_of(1, g))
    coef1 = pick(answer_b, 0, 0)
    back1 = pick(answer_b, 0, 1)
    coefficient_out[1] = coef1
    values1 = ex1 * payoff_of(1) + hold1 * fit(coef1, 1) + out1 * target1
    target0 = discount[0:1, :] * values1
    gather(part_c, gather_c, c_send, c_recv, 0, project(jnp.concatenate([in0 * target0, zero4], axis=0), 0))

    bar2 = discount[1:2, :] * (out1 * bar1 + in1 * fit(back1, 1))
    node_total = node_total + node_sum(ex2 * bar2, 2)
    node_one[me] = jnp.concatenate([node_total[:, 128 * k : 128 * k + 128] for k in range(8)], axis=0)

    def one_copy(k):
        return remote(
            node_one.at[me], node_one.at[me], n1_send.at[k - 1], n1_recv.at[me], path_id((me + k) % 16)
        )

    def one_arrival(k):
        p = (me + k) % 16
        return remote(node_one.at[me], node_one.at[p], n1_send.at[0], n1_recv.at[p], path_id(p))

    def two_copy(k):
        return remote(
            node_two.at[tme], node_two.at[tme], n2_send.at[k - 1], n2_recv.at[tme], trade_id((tme + k) % 8)
        )

    def two_arrival(k):
        t = (tme + k) % 8
        return remote(node_two.at[tme], node_two.at[t], n2_send.at[0], n2_recv.at[t], trade_id(t))

    run(1, 16, lambda k: one_copy(k).start())

    @pl.when(z == 0)
    def _():
        answer = solve(gathered(part_c, gather_c, c_send, c_recv))
        broadcast_done(answer_a, a_send, a_recv, 4 + mine)
        answer_src[...] = answer
        answer_c[mine] = answer
        broadcast(answer_c, cc_send, cc_recv, mine)

    run(1, 16, lambda k: one_arrival(k).wait_recv())
    total = node_one[0]
    for p in range(1, 16):
        total = total + node_one[p]
    node_two[tme] = total
    run(1, 8, lambda k: two_copy(k).start())

    for g in range(4):
        collect(answer_c, cc_send, cc_recv, g, owner_of(0, g))
    coef0 = pick(answer_c, 0, 0)
    coefficient_out[0] = coef0
    values_out[...] = ex0 * payoff_of(0) + hold0 * fit(coef0, 0) + out0 * target0

    run(1, 8, lambda k: two_arrival(k).wait_recv())
    total = node_two[0]
    for t in range(1, 8):
        total = total + node_two[t]
    grid = (
        lax.broadcasted_iota(jnp.int32, (8, 128), 0) * 128 + lax.broadcasted_iota(jnp.int32, (8, 128), 1)
    ).astype(F32)
    adjoint = -((grid + 1.0) * (horizon / NODES)) * total
    node_out[...] = adjoint
    line = jnp.concatenate([adjoint[k : k + 1, :] for k in range(8)], axis=1)
    bucket_out[...] = dot(jnp.broadcast_to(line, (8, NODES)), bucket_map[...], NT, HIGH)

    for i in (0, 2, 4):
        owner_copy(i).wait_send()
    for i in (1, 3, 5):

        @pl.when(z != DATES[i // 2])
        def _():
            owner_copy(i).wait_send()

    gather_sent(part_b, gather_b, b_send, b_recv, 1)
    gather_sent(part_c, gather_c, c_send, c_recv, 0)

    @pl.when(z == 2)
    def _():
        broadcast_done(answer_a, a_send, a_recv, mine)

    @pl.when(z == 1)
    def _():
        broadcast_done(answer_b, bb_send, bb_recv, mine)

    @pl.when(z == 0)
    def _():
        broadcast_done(answer_c, cc_send, cc_recv, mine)

    run(1, 16, lambda k: one_copy(k).wait_send())
    run(1, 8, lambda k: two_copy(k).wait_send())


def finish(values, coefficients, node, bucketed, values_out, coefficients_out, node_out, bucketed_out):
    values_out[...] = values[...]
    coefficients_out[...] = coefficients[...]
    node_out[...] = node[...].reshape(NODES)
    bucketed_out[...] = bucketed[0:1, :].reshape(64)


def shards(
    state,
    basis_projection_weight,
    factor_node_loading,
    curve,
    discount,
    region,
    carry_in,
    group_of,
    swap_start,
    swap_length,
    strike,
    notional,
    bucket_map,
):
    vmem = pl.BlockSpec(memory_space=pltpu.VMEM)
    dma = pltpu.SemaphoreType.DMA
    values, coefficients, node, bucketed = pl.pallas_call(
        kernel,
        out_shape=(
            jax.ShapeDtypeStruct((GRP, LOCAL), F32),
            jax.ShapeDtypeStruct((EXD, GRP, BASIS), F32),
            jax.ShapeDtypeStruct((8, 128), F32),
            jax.ShapeDtypeStruct((8, 64), F32),
        ),
        in_specs=[vmem] * 13,
        out_specs=(vmem,) * 4,
        scratch_shapes=[
            pltpu.VMEM((EXD, BASIS, LOCAL), BF16),
            pltpu.VMEM((EXD, 8, BASIS), F32),
            pltpu.VMEM((6, ROWS, 128), F32),
            pltpu.VMEM((6, ROWS, 128), F32),
            pltpu.VMEM((6, ROWS, 128), F32),
            pltpu.VMEM((8, ROWS, 128), F32),
            pltpu.VMEM((EXD * LOCAL, NODES), BF16),
            pltpu.VMEM((EXD * LOCAL, NODES), BF16),
            pltpu.VMEM((8, TPAD), jnp.int32),
            pltpu.VMEM((8, TPAD), F32),
            pltpu.VMEM((12, GRP, 256), F32),
            pltpu.VMEM((BASIS, BASIS), F32),
            pltpu.VMEM((2, BASIS), F32),
            pltpu.VMEM((8, 2, BASIS), F32),
            pltpu.VMEM((4, 2, BASIS), F32),
            pltpu.VMEM((4, 2, BASIS), F32),
            pltpu.VMEM((4, 2, BASIS), F32),
            pltpu.VMEM((4, 2, BASIS), F32),
            pltpu.VMEM((16, 2, BASIS), F32),
            pltpu.VMEM((16, 2, BASIS), F32),
            pltpu.VMEM((16, 8, 128), F32),
            pltpu.VMEM((8, 8, 128), F32),
            dma((6,)),
            dma((6,)),
            dma((6,)),
            dma((8,)),
            dma((15,)),
            dma((8,)),
            dma((4,)),
            dma((16,)),
            dma((15,)),
            dma((4,)),
            dma((4,)),
            dma((16,)),
            dma((15,)),
            dma((4,)),
            dma((15,)),
            dma((16,)),
            dma((7,)),
            dma((8,)),
        ],
        compiler_params=pltpu.CompilerParams(collective_id=0, has_side_effects=True),
        name="backward_window",
    )(
        state.reshape(EXD * LOCAL, FAC),
        basis_projection_weight,
        factor_node_loading,
        curve.reshape(1, NODES),
        discount,
        region.transpose(0, 2, 1),
        carry_in.T,
        group_of,
        swap_start,
        swap_length,
        strike,
        notional,
        bucket_map.T,
    )
    values, coefficients, node, bucketed = pl.pallas_call(
        finish,
        out_shape=(
            jax.ShapeDtypeStruct((GRP, LOCAL), F32),
            jax.ShapeDtypeStruct((EXD, GRP, BASIS), F32),
            jax.ShapeDtypeStruct((NODES,), F32),
            jax.ShapeDtypeStruct((64,), F32),
        ),
        in_specs=[vmem] * 4,
        out_specs=(vmem,) * 4,
        name="finish",
    )(values, coefficients, node, bucketed)
    return (values.T, coefficients, node, bucketed)


def solution(mesh):
    torus = Mesh(
        mesh.devices.reshape(2, 4, 2, 2, 4), ("path_0", "path_1", "path_2", "trade_0", "trade_1")
    )
    in_specs = (
        P(None, PATH, None),
        P(),
        P(),
        P(),
        P(None, PATH),
        P(None, PATH, TRADE),
        P(PATH, TRADE),
        P(TRADE),
        P(TRADE),
        P(TRADE),
        P(TRADE),
        P(TRADE),
        P(),
    )
    out_specs = (P(PATH, TRADE), P(None, TRADE, None), P(), P())
    return jax.shard_map(
        shards, mesh=torus, in_specs=in_specs, out_specs=out_specs, check_vma=False
    )
```

```python
import jax
import jax.numpy as jnp
from jax import lax
from jax.experimental import pallas as pl
from jax.experimental.pallas import tpu as pltpu
from jax.sharding import Mesh
from jax.sharding import PartitionSpec as P

EXD = 3
BASIS = 256
NODES = 1024
FAC = 128
GRP = 4
LOCAL = 1024
TRADES = 2500
TPAD = 2560
PATHS = 16384
PATH = ("path_0", "path_1", "path_2")
TRADE = ("trade_0", "trade_1")
MESH = pl.DeviceIdType.MESH
HIGH = lax.Precision.HIGHEST
F32 = jnp.float32
BF16 = jnp.bfloat16
ROWS = 264
DATES = (2, 0, 1)
FAR_FIRST = (12, 13, 11, 4, 5, 3, 10, 14, 9, 15, 8, 6, 2, 7, 1)


def owner_z(d, j, core):
    return {2: (j + core) % 2, 0: 2 + (j + core) % 2, 1: (1 - core) * (1 + j) + core * 3 * j}[d]

ridge_share = 0.05
horizon = 30.0
BOUND = (BASIS + ridge_share) * PATHS

NT = (((1,), (1,)), ((), ()))
NN = (((1,), (0,)), ((), ()))


def dot(a, b, dims=NN, precision=None):
    return lax.dot_general(a, b, dims, precision=precision, preferred_element_type=F32)


def split3(x):
    one = x.astype(BF16).astype(F32)
    rest = x - one
    two = rest.astype(BF16).astype(F32)
    return one, two, (rest - two).astype(BF16).astype(F32)


def stack3(x):
    pieces = split3(x)
    return jnp.concatenate([*pieces, jnp.zeros_like(x)], axis=0).astype(BF16)


def polynomials():
    low, high = ridge_share * PATHS / BOUND, 1.0
    steps = []
    while not steps or high - 1.0 > 2e-6:
        width, middle = high - low, high + low
        scale = 2.0 * (middle / width) ** 2 - 1.0
        steps.append((8.0 * middle / width**2 / scale, 8.0 / width**2 / scale))
        low, high = 1.0 - 1.0 / scale, 1.0 + 1.0 / scale
    return steps


def dot3(a, b):
    a_hi, b_hi = a.astype(BF16), b.astype(BF16)
    a_lo = (a - a_hi.astype(F32)).astype(BF16)
    b_lo = (b - b_hi.astype(F32)).astype(BF16)
    return dot(a_hi, b_hi) + (dot(a_hi, b_lo) + dot(a_lo, b_hi))


def invert(a):
    eye = (
        lax.broadcasted_iota(jnp.int32, (BASIS, BASIS), 0) == lax.broadcasted_iota(jnp.int32, (BASIS, BASIS), 1)
    ).astype(F32)
    a = a * (1.0 / BOUND)
    (alpha, beta), *others, near, last = polynomials()
    inverse = alpha * eye - beta * a
    product = dot3(a, inverse)
    for alpha, beta in others:
        both = dot3(jnp.concatenate([inverse, product], axis=0), alpha * eye - beta * product)
        inverse, product = both[:BASIS], both[BASIS:]
    alpha, beta = near
    inverse = dot3(inverse, alpha * eye - beta * product)
    alpha, beta = last
    rest = dot(a, inverse, NN, HIGH) - eye
    return ((alpha - beta) * inverse - beta * dot3(inverse, rest)) * (1.0 / BOUND)


def kernel(
    state_hbm,
    weight,
    loading_hbm,
    curve,
    discount,
    region,
    carry,
    group_of,
    swap_start,
    swap_length,
    strike,
    notional,
    bucket_hbm,
    values_out,
    coefficient_out,
    node_out,
    bucket_out,
    ft,
    rhs,
    away,
    home,
    got_core,
    got,
    state,
    loading,
    bucket_map,
    df_hi,
    df_lo,
    ints,
    floats,
    payoff,
    inverse_ref,
    answer_src,
    answer_a,
    answer_b,
    answer_c,
    part_b,
    part_c,
    gather_b,
    gather_c,
    node_one,
    node_two,
    core_send,
    core_recv,
    owner_send,
    owner_recv,
    load_sem,
    a_send,
    a_recv,
    b_send,
    b_recv,
    bb_send,
    bb_recv,
    c_send,
    c_recv,
    cc_send,
    cc_recv,
    n1_send,
    n1_recv,
    n2_send,
    n2_recv,
):
    yh = lax.axis_index("path_0")
    z = lax.axis_index("path_1")
    core = lax.axis_index("path_2")
    yl = lax.axis_index("trade_0")
    x = lax.axis_index("trade_1")
    me = yh * 8 + z * 2 + core
    tme = yl * 4 + x
    mine = core * 2 + yh
    owns = {d: z == owner_z(d, yh, core) for d in range(EXD)}

    def path_id(p):
        return {"path_0": p // 8, "path_1": (p // 2) % 4, "path_2": p % 2}

    def trade_id(t):
        return {"trade_0": t // 4, "trade_1": t % 4}

    def remote(src, dst, send, recv, device):
        return pltpu.make_async_remote_copy(
            src_ref=src, dst_ref=dst, send_sem=send, recv_sem=recv, device_id=device, device_id_type=MESH
        )

    def load_state(d):
        rows = pl.ds(d * LOCAL, LOCAL)
        return pltpu.make_async_copy(state_hbm.at[rows], state.at[rows], load_sem.at[d])

    def load_other(k):
        pair = ((loading_hbm, loading), (bucket_hbm, bucket_map))[k]
        return pltpu.make_async_copy(*pair, load_sem.at[3 + k])

    for d in DATES:
        load_state(d).start()
    load_other(0).start()
    load_other(1).start()

    barrier = pltpu.get_barrier_semaphore()
    for k in range(1, 16):
        pl.semaphore_signal(barrier, inc=1, device_id=path_id((me + k) % 16), device_id_type=MESH)
    for k in range(1, 8):
        pl.semaphore_signal(barrier, inc=1, device_id=trade_id((tme + k) % 8), device_id_type=MESH)

    weight_t = weight[...].T

    def features(d):
        load_state(d).wait()
        for c in range(4):
            chunk = state[d * LOCAL + c * 256 : d * LOCAL + c * 256 + 256, :]
            ft[d, :, c * 256 : c * 256 + 256] = jnp.tanh(dot(weight_t, chunk, NT)).astype(BF16)

    def masks(d):
        r = region[d]
        return (
            (r >= 1).astype(F32),
            (r == 1).astype(F32),
            (r == 2).astype(F32),
            (r == 0).astype(F32),
        )

    def project(rows8, d):
        return dot(rows8.astype(BF16), ft[d], NT)

    zero4 = jnp.zeros((4, LOCAL), F32)
    bar0 = jnp.full((4, LOCAL), 1.0 / PATHS, F32)
    target2 = discount[2:3, :] * carry[...]
    in0, hold0, ex0, out0 = masks(0)
    in1, hold1, ex1, out1 = masks(1)
    in2, hold2, ex2, out2 = masks(2)

    r128 = lax.broadcasted_iota(jnp.int32, (128, 128), 0)
    c128 = lax.broadcasted_iota(jnp.int32, (128, 128), 1)

    def pack(out, slot, top, low, right):
        last = low[:, 128:256]
        out[slot, 0:128, :] = jnp.where(r128 >= c128, top, last)
        out[slot, 128:256, :] = low[:, 0:128]
        diagonal = jnp.sum(jnp.where(r128 == c128, last, 0.0), axis=0, keepdims=True)
        out[slot, 256:264, :] = jnp.concatenate(
            [diagonal, right[:, 0:128], right[:, 128:256], jnp.zeros((5, 128), F32)], axis=0
        )

    def grams(slot):
        d = DATES[slot // 2]
        j = yh if slot % 2 else 1 - yh
        f = ft[d]
        theirs = (1 - core) * 2 + j
        ours = core * 2 + j
        one = f * jnp.where(region[d, pl.ds(theirs, 1), :] >= 1, 1.0, 0.0).astype(BF16)
        two = f * jnp.where(region[d, pl.ds(ours, 1), :] >= 1, 1.0, 0.0).astype(BF16)
        top = dot(jnp.concatenate([one[0:128], two[0:128]], axis=0), f[0:128], NT)
        low = dot(jnp.concatenate([one[128:256], two[128:256]], axis=0), f, NT)
        pack(away, slot, top[0:128], low[0:128], rhs[d, pl.ds(theirs, 1), :])
        pack(home, slot, top[128:256], low[128:256], rhs[d, pl.ds(ours, 1), :])

    def core_copy(i):
        return remote(away.at[i], got_core.at[i], core_send.at[i], core_recv.at[i], {"path_2": 1 - core})

    def owner_copy(i):
        other = 1 - i % 2
        j = 1 - yh if other else yh
        goal = owner_z(DATES[i // 2], j, core)
        at = 4 * other + (z - goal + 4) % 4
        to = {"path_0": j, "path_1": goal}
        return remote(home.at[i], got.at[at], owner_send.at[i], owner_recv.at[at], to)

    def combine(i):
        core_copy(i).wait()
        home[i] = home[i] + got_core[i]
        if i % 2:

            @pl.when(z != owner_z(DATES[i // 2], yh, core))
            def _():
                owner_copy(i).start()

        else:
            owner_copy(i).start()

    rhs[1] = jnp.zeros((8, BASIS), F32)
    features(2)
    rhs[2] = project(jnp.concatenate([in2 * target2, zero4], axis=0), 2)
    grams(0)
    grams(1)
    features(0)
    rhs[0] = project(jnp.concatenate([hold0 * bar0, zero4], axis=0), 0)
    grams(2)
    grams(3)
    pl.semaphore_wait(barrier, 22)
    for i in range(4):
        core_copy(i).start()
    features(1)
    grams(4)
    core_copy(4).start()
    for i in range(4):
        combine(i)
    grams(5)
    core_copy(5).start()

    combine(4)
    combine(5)

    ints[...] = jnp.zeros_like(ints)
    floats[...] = jnp.zeros_like(floats)
    starts, amounts = swap_start[...].reshape(1, TRADES), notional[...].reshape(1, TRADES)
    ints[0:1, 0:TRADES] = group_of[...].reshape(1, TRADES) - tme * GRP
    ints[1:2, 0:TRADES] = starts
    ints[2:3, 0:TRADES] = starts + swap_length[...].reshape(1, TRADES)
    floats[0:1, 0:TRADES] = amounts
    floats[1:2, 0:TRADES] = amounts * (strike[...].reshape(1, TRADES) * (horizon / NODES))
    i32 = lax.broadcasted_iota(jnp.int32, (32, 512), 0)
    i128 = lax.broadcasted_iota(jnp.int32, (128, 512), 0)

    def histogram(i, total):
        span = pl.ds(pl.multiple_of(i * 512, 512), 512)
        group = ints[0:1, span]
        pieces = [*split3(floats[0:1, span]), *split3(floats[1:2, span])]
        for row, sign in ((1, 1.0), (2, -1.0)):
            key = ints[row : row + 1, span]
            hit = i32 == (key // 128) * 4 + group
            left = jnp.concatenate([jnp.where(hit, sign * piece, 0.0) for piece in pieces], axis=0).astype(BF16)
            right = (i128 == key % 128).astype(F32).astype(BF16)
            total = total + dot(left, right, NT)
        return total

    table = lax.fori_loop(0, 5, histogram, jnp.zeros((192, 128), F32))
    steps = table[0:32] + table[32:64] + table[64:96]
    slopes = table[96:128] + table[128:160] + table[160:192]
    before = (r128 < c128).astype(F32)
    ra = lax.broadcasted_iota(jnp.int32, (32, 32), 0)
    ca = lax.broadcasted_iota(jnp.int32, (32, 32), 1)
    earlier = ((ca // 4 < ra // 4) & (ca % 4 == ra % 4)).astype(F32)
    coupon = dot(slopes, before, NN, HIGH) + jnp.sum(dot(earlier, slopes, NN, HIGH), axis=1, keepdims=True)
    flat = steps - coupon
    cash = jnp.concatenate([flat[4 * a : 4 * a + 4, :] for a in range(8)], axis=1)
    cash_stack = stack3(cash)

    times = (lax.broadcasted_iota(jnp.int32, (1, NODES), 1).astype(F32) + 1.0) * (horizon / NODES)
    curve_row = curve[...]

    def sum3(t):
        return t[0:4] + t[4:8] + t[8:12]

    def discounting(first, last):
        def chunk(i, _):
            span = pl.ds(pl.multiple_of(i * 256, 256), 256)
            shock = dot(state[span, :], loading[...])
            factor = jnp.exp(-times * (curve_row + shock))
            hi = factor.astype(BF16)
            lo = (factor - hi.astype(F32)).astype(BF16)
            df_hi[span, :] = hi
            df_lo[span, :] = lo
            payoff[i] = sum3(dot(cash_stack, hi, NT) + dot(cash_stack, lo, NT))
            return 0

        lax.fori_loop(first, last, chunk, 0)

    def node_sum(w, d):
        stack = stack3(w)
        span = pl.ds(d * LOCAL, LOCAL)
        t = sum3(dot(stack, df_hi[span, :]) + dot(stack, df_lo[span, :]))
        return jnp.sum(cash * t, axis=0, keepdims=True)

    load_other(0).wait()
    discounting(8, 12)

    discounting(0, 2)

    def solve(rows):
        return dot(rows, inverse_ref[...], NN, HIGH)

    def run(first, last, f):
        def go(k, _):
            f(k)
            return 0

        lax.fori_loop(first, last, go, 0)

    def answer_copy(k, dst, sends, recvs, at):
        return remote(answer_src, dst.at[at], sends.at[k - 1], recvs.at[at], path_id((me + k) % 16))

    def broadcast(dst, sends, recvs, at):
        for k in FAR_FIRST:
            answer_copy(k, dst, sends, recvs, at).start()

    def broadcast_done(dst, sends, recvs, at):
        run(1, 16, lambda k: answer_copy(k, dst, sends, recvs, at).wait_send())

    def collect(dst, sends, recvs, at, owner):
        @pl.when(me != owner)
        def _():
            remote(answer_src, dst.at[at], sends.at[0], recvs.at[at], path_id(owner)).wait_recv()

    def owner_of(d, g):
        return (g % 2) * 8 + owner_z(d, g % 2, g // 2) * 2 + g // 2

    for place, d in enumerate(DATES):

        @pl.when(owns[d])
        def _():
            packed = home[2 * place + 1]
            for at in range(1, 8):
                remote(home.at[0], got.at[at], owner_send.at[0], owner_recv.at[at], {"path_1": 0}).wait_recv()
                packed = packed + got[at]
            got[0] = packed

    @pl.when(owns[0] | owns[1] | owns[2])
    def _():
        packed = got[0]
        mix = packed[0:128]
        flip = mix.T
        b = packed[128:256]
        ridge = jnp.where(r128 == c128, ridge_share * PATHS, 0.0)
        a = jnp.where(r128 >= c128, mix, flip) + ridge
        c = jnp.where(r128 < c128, mix, jnp.where(r128 > c128, flip, packed[256:257])) + ridge
        full = jnp.concatenate(
            [jnp.concatenate([a, b.T], axis=1), jnp.concatenate([b, c], axis=1)], axis=0
        )
        inverse_ref[...] = invert(full)

        row = jnp.concatenate([packed[257:258], packed[258:259]], axis=1)
        answer_src[...] = solve(jnp.broadcast_to(row, (2, BASIS)))

    for base, d in ((0, 2), (4, 0)):

        @pl.when(owns[d])
        def _():
            broadcast(answer_a, a_send, a_recv, base + mine)
            answer_a[base + mine] = answer_src[...]

    discounting(4, 8)

    for g in range(4):
        collect(answer_a, a_send, a_recv, g, owner_of(2, g))
        collect(answer_a, a_send, a_recv, 4 + g, owner_of(0, g))

    def pick(buffer, base, row):
        return jnp.concatenate([buffer[base + g, row : row + 1, :] for g in range(4)], axis=0)

    def payoff_of(d):
        return jnp.concatenate([payoff[4 * d + k] for k in range(4)], axis=1)

    def fit(coefficient, d):
        stacked = jnp.concatenate([coefficient, jnp.zeros_like(coefficient)], axis=0).astype(BF16)
        return dot(stacked, ft[d])[0:4]

    coef2 = pick(answer_a, 0, 0)
    back0 = pick(answer_a, 4, 0)
    coefficient_out[2] = coef2
    values2 = ex2 * payoff_of(2) + hold2 * fit(coef2, 2) + out2 * target2
    bar1 = discount[0:1, :] * (out0 * bar0 + in0 * fit(back0, 0))
    target1 = discount[1:2, :] * values2

    def gather_copy(src, dst, sends, recvs, d, g):
        return remote(src.at[g], dst.at[me], sends.at[g], recvs.at[me], path_id(owner_of(d, g)))

    def gather(src, dst, sends, recvs, d, rows8):
        for g in range(4):
            src[g] = jnp.concatenate([rows8[g : g + 1], rows8[4 + g : 5 + g]], axis=0)
        for g in range(4):

            @pl.when(me != owner_of(d, g))
            def _():
                gather_copy(src, dst, sends, recvs, d, g).start()

        @pl.when(owns[d])
        def _():
            dst[me] = src[mine]

    def gather_sent(src, dst, sends, recvs, d):
        for g in range(4):

            @pl.when(me != owner_of(d, g))
            def _():
                gather_copy(src, dst, sends, recvs, d, g).wait_send()

    def gathered(src, dst, sends, recvs):
        def arrival(k):
            p = (me + k) % 16
            remote(src.at[0], dst.at[p], sends.at[0], recvs.at[p], path_id(p)).wait_recv()

        run(1, 16, arrival)
        total = dst[0]
        for p in range(1, 16):
            total = total + dst[p]
        return total

    gather(
        part_b, gather_b, b_send, b_recv, 1, project(jnp.concatenate([in1 * target1, hold1 * bar1], axis=0), 1)
    )
    discounting(2, 4)
    node_total = node_sum(ex0 * bar0, 0) + node_sum(ex1 * bar1, 1)

    @pl.when(owns[1])
    def _():
        answer = solve(gathered(part_b, gather_b, b_send, b_recv))
        answer_src[...] = answer
        answer_b[mine] = answer
        broadcast(answer_b, bb_send, bb_recv, mine)

    for g in range(4):
        collect(answer_b, bb_send, bb_recv, g, owner_of(1, g))
    coef1 = pick(answer_b, 0, 0)
    back1 = pick(answer_b, 0, 1)
    coefficient_out[1] = coef1
    values1 = ex1 * payoff_of(1) + hold1 * fit(coef1, 1) + out1 * target1
    target0 = discount[0:1, :] * values1
    gather(part_c, gather_c, c_send, c_recv, 0, project(jnp.concatenate([in0 * target0, zero4], axis=0), 0))

    bar2 = discount[1:2, :] * (out1 * bar1 + in1 * fit(back1, 1))
    node_total = node_total + node_sum(ex2 * bar2, 2)
    node_one[me] = jnp.concatenate([node_total[:, 128 * k : 128 * k + 128] for k in range(8)], axis=0)

    def one_copy(k):
        return remote(
            node_one.at[me], node_one.at[me], n1_send.at[k - 1], n1_recv.at[me], path_id((me + k) % 16)
        )

    def one_arrival(k):
        p = (me + k) % 16
        return remote(node_one.at[me], node_one.at[p], n1_send.at[0], n1_recv.at[p], path_id(p))

    def two_copy(k):
        return remote(
            node_two.at[tme], node_two.at[tme], n2_send.at[k - 1], n2_recv.at[tme], trade_id((tme + k) % 8)
        )

    def two_arrival(k):
        t = (tme + k) % 8
        return remote(node_two.at[tme], node_two.at[t], n2_send.at[0], n2_recv.at[t], trade_id(t))

    run(1, 16, lambda k: one_copy(k).start())

    @pl.when(owns[0])
    def _():
        answer = solve(gathered(part_c, gather_c, c_send, c_recv))
        broadcast_done(answer_a, a_send, a_recv, 4 + mine)
        answer_src[...] = answer
        answer_c[mine] = answer
        broadcast(answer_c, cc_send, cc_recv, mine)

    run(1, 16, lambda k: one_arrival(k).wait_recv())
    total = node_one[0]
    for p in range(1, 16):
        total = total + node_one[p]
    node_two[tme] = total
    run(1, 8, lambda k: two_copy(k).start())

    for g in range(4):
        collect(answer_c, cc_send, cc_recv, g, owner_of(0, g))
    coef0 = pick(answer_c, 0, 0)
    coefficient_out[0] = coef0
    values_out[...] = ex0 * payoff_of(0) + hold0 * fit(coef0, 0) + out0 * target0

    run(1, 8, lambda k: two_arrival(k).wait_recv())
    total = node_two[0]
    for t in range(1, 8):
        total = total + node_two[t]
    grid = (
        lax.broadcasted_iota(jnp.int32, (8, 128), 0) * 128 + lax.broadcasted_iota(jnp.int32, (8, 128), 1)
    ).astype(F32)
    adjoint = -((grid + 1.0) * (horizon / NODES)) * total
    node_out[...] = adjoint
    load_other(1).wait()
    line = jnp.concatenate([adjoint[k : k + 1, :] for k in range(8)], axis=1)
    bucket_out[...] = dot(jnp.broadcast_to(line, (8, NODES)), bucket_map[...], NT, HIGH)

    for i in (0, 2, 4):
        owner_copy(i).wait_send()
    for i in (1, 3, 5):

        @pl.when(z != owner_z(DATES[i // 2], yh, core))
        def _():
            owner_copy(i).wait_send()

    gather_sent(part_b, gather_b, b_send, b_recv, 1)
    gather_sent(part_c, gather_c, c_send, c_recv, 0)

    @pl.when(owns[2])
    def _():
        broadcast_done(answer_a, a_send, a_recv, mine)

    @pl.when(owns[1])
    def _():
        broadcast_done(answer_b, bb_send, bb_recv, mine)

    @pl.when(owns[0])
    def _():
        broadcast_done(answer_c, cc_send, cc_recv, mine)

    run(1, 16, lambda k: one_copy(k).wait_send())
    run(1, 8, lambda k: two_copy(k).wait_send())


def finish(values, coefficients, node, bucketed, values_out, coefficients_out, node_out, bucketed_out):
    values_out[...] = values[...]
    coefficients_out[...] = coefficients[...]
    node_out[...] = node[...].reshape(NODES)
    bucketed_out[...] = bucketed[0:1, :].reshape(64)


def shards(
    state,
    basis_projection_weight,
    factor_node_loading,
    curve,
    discount,
    region,
    carry_in,
    group_of,
    swap_start,
    swap_length,
    strike,
    notional,
    bucket_map,
):
    vmem = pl.BlockSpec(memory_space=pltpu.VMEM)
    anywhere = pl.BlockSpec(memory_space=pl.ANY)
    dma = pltpu.SemaphoreType.DMA
    values, coefficients, node, bucketed = pl.pallas_call(
        kernel,
        out_shape=(
            jax.ShapeDtypeStruct((GRP, LOCAL), F32),
            jax.ShapeDtypeStruct((EXD, GRP, BASIS), F32),
            jax.ShapeDtypeStruct((8, 128), F32),
            jax.ShapeDtypeStruct((8, 64), F32),
        ),
        in_specs=[anywhere, vmem, anywhere, *[vmem] * 9, anywhere],
        out_specs=(vmem,) * 4,
        scratch_shapes=[
            pltpu.VMEM((EXD, BASIS, LOCAL), BF16),
            pltpu.VMEM((EXD, 8, BASIS), F32),
            pltpu.VMEM((6, ROWS, 128), F32),
            pltpu.VMEM((6, ROWS, 128), F32),
            pltpu.VMEM((6, ROWS, 128), F32),
            pltpu.VMEM((8, ROWS, 128), F32),
            pltpu.VMEM((EXD * LOCAL, FAC), BF16),
            pltpu.VMEM((FAC, NODES), BF16),
            pltpu.VMEM((64, NODES), F32),
            pltpu.VMEM((EXD * LOCAL, NODES), BF16),
            pltpu.VMEM((EXD * LOCAL, NODES), BF16),
            pltpu.VMEM((8, TPAD), jnp.int32),
            pltpu.VMEM((8, TPAD), F32),
            pltpu.VMEM((12, GRP, 256), F32),
            pltpu.VMEM((BASIS, BASIS), F32),
            pltpu.VMEM((2, BASIS), F32),
            pltpu.VMEM((8, 2, BASIS), F32),
            pltpu.VMEM((4, 2, BASIS), F32),
            pltpu.VMEM((4, 2, BASIS), F32),
            pltpu.VMEM((4, 2, BASIS), F32),
            pltpu.VMEM((4, 2, BASIS), F32),
            pltpu.VMEM((16, 2, BASIS), F32),
            pltpu.VMEM((16, 2, BASIS), F32),
            pltpu.VMEM((16, 8, 128), F32),
            pltpu.VMEM((8, 8, 128), F32),
            dma((6,)),
            dma((6,)),
            dma((6,)),
            dma((8,)),
            dma((5,)),
            dma((15,)),
            dma((8,)),
            dma((4,)),
            dma((16,)),
            dma((15,)),
            dma((4,)),
            dma((4,)),
            dma((16,)),
            dma((15,)),
            dma((4,)),
            dma((15,)),
            dma((16,)),
            dma((7,)),
            dma((8,)),
        ],
        compiler_params=pltpu.CompilerParams(collective_id=0, has_side_effects=True),
        name="backward_window",
    )(
        state.reshape(EXD * LOCAL, FAC),
        basis_projection_weight,
        factor_node_loading,
        curve.reshape(1, NODES),
        discount,
        region.transpose(0, 2, 1),
        carry_in.T,
        group_of,
        swap_start,
        swap_length,
        strike,
        notional,
        bucket_map.T,
    )
    values, coefficients, node, bucketed = pl.pallas_call(
        finish,
        out_shape=(
            jax.ShapeDtypeStruct((GRP, LOCAL), F32),
            jax.ShapeDtypeStruct((EXD, GRP, BASIS), F32),
            jax.ShapeDtypeStruct((NODES,), F32),
            jax.ShapeDtypeStruct((64,), F32),
        ),
        in_specs=[vmem] * 4,
        out_specs=(vmem,) * 4,
        name="finish",
    )(values, coefficients, node, bucketed)
    return (values.T, coefficients, node, bucketed)


def solution(mesh):
    torus = Mesh(
        mesh.devices.reshape(2, 4, 2, 2, 4), ("path_0", "path_1", "path_2", "trade_0", "trade_1")
    )
    in_specs = (
        P(None, PATH, None),
        P(),
        P(),
        P(),
        P(None, PATH),
        P(None, PATH, TRADE),
        P(PATH, TRADE),
        P(TRADE),
        P(TRADE),
        P(TRADE),
        P(TRADE),
        P(TRADE),
        P(),
    )
    out_specs = (P(PATH, TRADE), P(None, TRADE, None), P(), P())
    return jax.shard_map(
        shards, mesh=torus, in_specs=in_specs, out_specs=out_specs, check_vma=False
    )
```

```python
import jax
import jax.numpy as jnp
from jax import lax
from jax.experimental import pallas as pl
from jax.experimental.pallas import tpu as pltpu
from jax.sharding import Mesh
from jax.sharding import PartitionSpec as P

EXD = 3
BASIS = 256
NODES = 1024
FAC = 128
GRP = 4
LOCAL = 1024
TRADES = 2500
TPAD = 2560
PATHS = 16384
PATH = ("path_0", "path_1", "path_2")
TRADE = ("trade_0", "trade_1")
MESH = pl.DeviceIdType.MESH
HIGH = lax.Precision.HIGHEST
F32 = jnp.float32
BF16 = jnp.bfloat16
ROWS = 264
DATES = (2, 0, 1)
FAR_FIRST = (12, 13, 11, 4, 5, 3, 10, 14, 9, 15, 8, 6, 2, 7, 1)


def owner_z(d, j, core):
    return {2: (j + core) % 2, 0: 2 + (j + core) % 2, 1: (1 - core) * (1 + j) + core * 3 * j}[d]

ridge_share = 0.05
horizon = 30.0
BOUND = (BASIS + ridge_share) * PATHS

NT = (((1,), (1,)), ((), ()))
NN = (((1,), (0,)), ((), ()))


def dot(a, b, dims=NN, precision=None):
    return lax.dot_general(a, b, dims, precision=precision, preferred_element_type=F32)


def split3(x):
    one = x.astype(BF16).astype(F32)
    rest = x - one
    two = rest.astype(BF16).astype(F32)
    return one, two, (rest - two).astype(BF16).astype(F32)


def stack3(x):
    pieces = split3(x)
    return jnp.concatenate([*pieces, jnp.zeros_like(x)], axis=0).astype(BF16)


def polynomials():
    low, high = ridge_share * PATHS / BOUND, 1.0
    steps = []
    while not steps or high - 1.0 > 2e-6:
        width, middle = high - low, high + low
        scale = 2.0 * (middle / width) ** 2 - 1.0
        steps.append((8.0 * middle / width**2 / scale, 8.0 / width**2 / scale))
        low, high = 1.0 - 1.0 / scale, 1.0 + 1.0 / scale
    return steps


def dot3(a, b):
    a_hi, b_hi = a.astype(BF16), b.astype(BF16)
    a_lo = (a - a_hi.astype(F32)).astype(BF16)
    b_lo = (b - b_hi.astype(F32)).astype(BF16)
    return dot(a_hi, b_hi) + (dot(a_hi, b_lo) + dot(a_lo, b_hi))


def invert(a):
    eye = (
        lax.broadcasted_iota(jnp.int32, (BASIS, BASIS), 0) == lax.broadcasted_iota(jnp.int32, (BASIS, BASIS), 1)
    ).astype(F32)
    a = a * (1.0 / BOUND)
    (alpha, beta), *others, near, last = polynomials()
    inverse = alpha * eye - beta * a
    product = dot3(a, inverse)
    for alpha, beta in others:
        both = dot3(jnp.concatenate([inverse, product], axis=0), alpha * eye - beta * product)
        inverse, product = both[:BASIS], both[BASIS:]
    alpha, beta = near
    inverse = dot3(inverse, alpha * eye - beta * product)
    alpha, beta = last
    rest = dot(a, inverse, NN, HIGH) - eye
    return ((alpha - beta) * inverse - beta * dot3(inverse, rest)) * (1.0 / BOUND)


def kernel(
    state_hbm,
    weight,
    loading_hbm,
    curve,
    discount,
    region,
    carry,
    group_of,
    swap_start,
    swap_length,
    strike,
    notional,
    bucket_hbm,
    values_out,
    coefficient_out,
    node_out,
    bucket_out,
    ft,
    rhs,
    away,
    home,
    got_core,
    got,
    state,
    loading,
    bucket_map,
    df_hi,
    df_lo,
    ints,
    floats,
    payoff,
    inverse_ref,
    answer_src,
    answer_a,
    answer_b,
    answer_c,
    part_b,
    part_c,
    gather_b,
    gather_c,
    node_one,
    node_two,
    core_send,
    core_recv,
    owner_send,
    owner_recv,
    load_sem,
    a_send,
    a_recv,
    b_send,
    b_recv,
    bb_send,
    bb_recv,
    c_send,
    c_recv,
    cc_send,
    cc_recv,
    n1_send,
    n1_recv,
    n2_send,
    n2_recv,
):
    yh = lax.axis_index("path_0")
    z = lax.axis_index("path_1")
    core = lax.axis_index("path_2")
    yl = lax.axis_index("trade_0")
    x = lax.axis_index("trade_1")
    me = yh * 8 + z * 2 + core
    tme = yl * 4 + x
    mine = core * 2 + yh
    owns = {d: z == owner_z(d, yh, core) for d in range(EXD)}

    def path_id(p):
        return {"path_0": p // 8, "path_1": (p // 2) % 4, "path_2": p % 2}

    def trade_id(t):
        return {"trade_0": t // 4, "trade_1": t % 4}

    def remote(src, dst, send, recv, device):
        return pltpu.make_async_remote_copy(
            src_ref=src, dst_ref=dst, send_sem=send, recv_sem=recv, device_id=device, device_id_type=MESH
        )

    def load_state(d):
        rows = pl.ds(d * LOCAL, LOCAL)
        return pltpu.make_async_copy(state_hbm.at[rows], state.at[rows], load_sem.at[d])

    def load_other(k):
        pair = ((loading_hbm, loading), (bucket_hbm, bucket_map))[k]
        return pltpu.make_async_copy(*pair, load_sem.at[3 + k])

    for d in DATES:
        load_state(d).start()
    load_other(0).start()
    load_other(1).start()

    barrier = pltpu.get_barrier_semaphore()
    for k in range(1, 16):
        pl.semaphore_signal(barrier, inc=1, device_id=path_id((me + k) % 16), device_id_type=MESH)
    for k in range(1, 8):
        pl.semaphore_signal(barrier, inc=1, device_id=trade_id((tme + k) % 8), device_id_type=MESH)

    weight_t = weight[...].T

    def features(d):
        load_state(d).wait()
        for c in range(4):
            chunk = state[d * LOCAL + c * 256 : d * LOCAL + c * 256 + 256, :]
            ft[d, :, c * 256 : c * 256 + 256] = jnp.tanh(dot(weight_t, chunk, NT)).astype(BF16)

    def masks(d):
        r = region[d]
        return (
            (r >= 1).astype(F32),
            (r == 1).astype(F32),
            (r == 2).astype(F32),
            (r == 0).astype(F32),
        )

    def project(rows8, d):
        return dot(rows8.astype(BF16), ft[d], NT)

    zero4 = jnp.zeros((4, LOCAL), F32)
    bar0 = jnp.full((4, LOCAL), 1.0 / PATHS, F32)
    target2 = discount[2:3, :] * carry[...]
    in0, hold0, ex0, out0 = masks(0)
    in1, hold1, ex1, out1 = masks(1)
    in2, hold2, ex2, out2 = masks(2)

    r128 = lax.broadcasted_iota(jnp.int32, (128, 128), 0)
    c128 = lax.broadcasted_iota(jnp.int32, (128, 128), 1)

    def pack(out, slot, top, low, right):
        last = low[:, 128:256]
        out[slot, 0:128, :] = jnp.where(r128 >= c128, top, last)
        out[slot, 128:256, :] = low[:, 0:128]
        diagonal = jnp.sum(jnp.where(r128 == c128, last, 0.0), axis=0, keepdims=True)
        out[slot, 256:264, :] = jnp.concatenate(
            [diagonal, right[:, 0:128], right[:, 128:256], jnp.zeros((5, 128), F32)], axis=0
        )

    def grams(slot):
        d = DATES[slot // 2]
        j = yh if slot % 2 else 1 - yh
        f = ft[d]
        theirs = (1 - core) * 2 + j
        ours = core * 2 + j
        one = f * jnp.where(region[d, pl.ds(theirs, 1), :] >= 1, 1.0, 0.0).astype(BF16)
        two = f * jnp.where(region[d, pl.ds(ours, 1), :] >= 1, 1.0, 0.0).astype(BF16)
        top = dot(jnp.concatenate([one[0:128], two[0:128]], axis=0), f[0:128], NT)
        low = dot(jnp.concatenate([one[128:256], two[128:256]], axis=0), f, NT)
        pack(away, slot, top[0:128], low[0:128], rhs[d, pl.ds(theirs, 1), :])
        pack(home, slot, top[128:256], low[128:256], rhs[d, pl.ds(ours, 1), :])

    def core_copy(i):
        return remote(away.at[i], got_core.at[i], core_send.at[i], core_recv.at[i], {"path_2": 1 - core})

    def owner_copy(i):
        other = 1 - i % 2
        j = 1 - yh if other else yh
        goal = owner_z(DATES[i // 2], j, core)
        at = 4 * other + (z - goal + 4) % 4
        to = {"path_0": j, "path_1": goal}
        return remote(home.at[i], got.at[at], owner_send.at[i], owner_recv.at[at], to)

    def combine(i):
        core_copy(i).wait()
        home[i] = home[i] + got_core[i]
        if i % 2:

            @pl.when(z != owner_z(DATES[i // 2], yh, core))
            def _():
                owner_copy(i).start()

        else:
            owner_copy(i).start()

    rhs[1] = jnp.zeros((8, BASIS), F32)
    features(2)
    rhs[2] = project(jnp.concatenate([in2 * target2, zero4], axis=0), 2)
    grams(0)
    grams(1)
    features(0)
    rhs[0] = project(jnp.concatenate([hold0 * bar0, zero4], axis=0), 0)
    grams(2)
    grams(3)
    pl.semaphore_wait(barrier, 22)
    for i in range(4):
        core_copy(i).start()
    features(1)
    grams(4)
    core_copy(4).start()
    for i in range(4):
        combine(i)
    grams(5)
    core_copy(5).start()

    ints[...] = jnp.zeros_like(ints)
    floats[...] = jnp.zeros_like(floats)
    starts, amounts = swap_start[...].reshape(1, TRADES), notional[...].reshape(1, TRADES)
    ints[0:1, 0:TRADES] = group_of[...].reshape(1, TRADES) - tme * GRP
    ints[1:2, 0:TRADES] = starts
    ints[2:3, 0:TRADES] = starts + swap_length[...].reshape(1, TRADES)
    floats[0:1, 0:TRADES] = amounts
    floats[1:2, 0:TRADES] = amounts * (strike[...].reshape(1, TRADES) * (horizon / NODES))
    i32 = lax.broadcasted_iota(jnp.int32, (32, 512), 0)
    i128 = lax.broadcasted_iota(jnp.int32, (128, 512), 0)

    def histogram(i, total):
        span = pl.ds(pl.multiple_of(i * 512, 512), 512)
        group = ints[0:1, span]
        pieces = [*split3(floats[0:1, span]), *split3(floats[1:2, span])]
        for row, sign in ((1, 1.0), (2, -1.0)):
            key = ints[row : row + 1, span]
            hit = i32 == (key // 128) * 4 + group
            left = jnp.concatenate([jnp.where(hit, sign * piece, 0.0) for piece in pieces], axis=0).astype(BF16)
            right = (i128 == key % 128).astype(F32).astype(BF16)
            total = total + dot(left, right, NT)
        return total

    table = lax.fori_loop(0, 5, histogram, jnp.zeros((192, 128), F32))
    steps = table[0:32] + table[32:64] + table[64:96]
    slopes = table[96:128] + table[128:160] + table[160:192]
    before = (r128 < c128).astype(F32)
    ra = lax.broadcasted_iota(jnp.int32, (32, 32), 0)
    ca = lax.broadcasted_iota(jnp.int32, (32, 32), 1)
    earlier = ((ca // 4 < ra // 4) & (ca % 4 == ra % 4)).astype(F32)
    coupon = dot(slopes, before, NN, HIGH) + jnp.sum(dot(earlier, slopes, NN, HIGH), axis=1, keepdims=True)
    flat = steps - coupon
    cash = jnp.concatenate([flat[4 * a : 4 * a + 4, :] for a in range(8)], axis=1)
    cash_stack = stack3(cash)

    times = (lax.broadcasted_iota(jnp.int32, (1, NODES), 1).astype(F32) + 1.0) * (horizon / NODES)
    curve_row = curve[...]

    def sum3(t):
        return t[0:4] + t[4:8] + t[8:12]

    def discounting(first, last):
        def chunk(i, _):
            span = pl.ds(pl.multiple_of(i * 256, 256), 256)
            shock = dot(state[span, :], loading[...])
            factor = jnp.exp(-times * (curve_row + shock))
            hi = factor.astype(BF16)
            lo = (factor - hi.astype(F32)).astype(BF16)
            df_hi[span, :] = hi
            df_lo[span, :] = lo
            payoff[i] = sum3(dot(cash_stack, hi, NT) + dot(cash_stack, lo, NT))
            return 0

        lax.fori_loop(first, last, chunk, 0)

    def node_sum(w, d):
        stack = stack3(w)
        span = pl.ds(d * LOCAL, LOCAL)
        t = sum3(dot(stack, df_hi[span, :]) + dot(stack, df_lo[span, :]))
        return jnp.sum(cash * t, axis=0, keepdims=True)

    load_other(0).wait()
    discounting(8, 12)

    discounting(0, 2)
    combine(4)
    combine(5)

    def solve(rows):
        return dot(rows, inverse_ref[...], NN, HIGH)

    def run(first, last, f):
        def go(k, _):
            f(k)
            return 0

        lax.fori_loop(first, last, go, 0)

    def answer_copy(k, dst, sends, recvs, at):
        return remote(answer_src, dst.at[at], sends.at[k - 1], recvs.at[at], path_id((me + k) % 16))

    def broadcast(dst, sends, recvs, at):
        for k in FAR_FIRST:
            answer_copy(k, dst, sends, recvs, at).start()

    def broadcast_done(dst, sends, recvs, at):
        run(1, 16, lambda k: answer_copy(k, dst, sends, recvs, at).wait_send())

    def collect(dst, sends, recvs, at, owner):
        @pl.when(me != owner)
        def _():
            remote(answer_src, dst.at[at], sends.at[0], recvs.at[at], path_id(owner)).wait_recv()

    def owner_of(d, g):
        return (g % 2) * 8 + owner_z(d, g % 2, g // 2) * 2 + g // 2

    def arrive(place):
        packed = home[2 * place + 1]
        for at in range(1, 8):
            remote(home.at[0], got.at[at], owner_send.at[0], owner_recv.at[at], {"path_1": 0}).wait_recv()
            packed = packed + got[at]
        got[0] = packed

    def invert_sum():
        packed = got[0]
        mix = packed[0:128]
        flip = mix.T
        b = packed[128:256]
        ridge = jnp.where(r128 == c128, ridge_share * PATHS, 0.0)
        a = jnp.where(r128 >= c128, mix, flip) + ridge
        c = jnp.where(r128 < c128, mix, jnp.where(r128 > c128, flip, packed[256:257])) + ridge
        full = jnp.concatenate(
            [jnp.concatenate([a, b.T], axis=1), jnp.concatenate([b, c], axis=1)], axis=0
        )
        inverse_ref[...] = invert(full)

    for place in range(2):

        @pl.when(owns[DATES[place]])
        def _():
            arrive(place)

    @pl.when(owns[0] | owns[2])
    def _():
        invert_sum()
        row = jnp.concatenate([got[0, 257:258], got[0, 258:259]], axis=1)
        answer_src[...] = solve(jnp.broadcast_to(row, (2, BASIS)))

    for base, d in ((0, 2), (4, 0)):

        @pl.when(owns[d])
        def _():
            broadcast(answer_a, a_send, a_recv, base + mine)
            answer_a[base + mine] = answer_src[...]

    discounting(4, 8)

    @pl.when(owns[1])
    def _():
        arrive(2)
        invert_sum()

    for g in range(4):
        collect(answer_a, a_send, a_recv, g, owner_of(2, g))
        collect(answer_a, a_send, a_recv, 4 + g, owner_of(0, g))

    def pick(buffer, base, row):
        return jnp.concatenate([buffer[base + g, row : row + 1, :] for g in range(4)], axis=0)

    def payoff_of(d):
        return jnp.concatenate([payoff[4 * d + k] for k in range(4)], axis=1)

    def fit(coefficient, d):
        stacked = jnp.concatenate([coefficient, jnp.zeros_like(coefficient)], axis=0).astype(BF16)
        return dot(stacked, ft[d])[0:4]

    coef2 = pick(answer_a, 0, 0)
    back0 = pick(answer_a, 4, 0)
    coefficient_out[2] = coef2
    values2 = ex2 * payoff_of(2) + hold2 * fit(coef2, 2) + out2 * target2
    bar1 = discount[0:1, :] * (out0 * bar0 + in0 * fit(back0, 0))
    target1 = discount[1:2, :] * values2

    def gather_copy(src, dst, sends, recvs, d, g):
        return remote(src.at[g], dst.at[me], sends.at[g], recvs.at[me], path_id(owner_of(d, g)))

    def gather(src, dst, sends, recvs, d, rows8):
        for g in range(4):
            src[g] = jnp.concatenate([rows8[g : g + 1], rows8[4 + g : 5 + g]], axis=0)
        for g in range(4):

            @pl.when(me != owner_of(d, g))
            def _():
                gather_copy(src, dst, sends, recvs, d, g).start()

        @pl.when(owns[d])
        def _():
            dst[me] = src[mine]

    def gather_sent(src, dst, sends, recvs, d):
        for g in range(4):

            @pl.when(me != owner_of(d, g))
            def _():
                gather_copy(src, dst, sends, recvs, d, g).wait_send()

    def gathered(src, dst, sends, recvs):
        def arrival(k):
            p = (me + k) % 16
            remote(src.at[0], dst.at[p], sends.at[0], recvs.at[p], path_id(p)).wait_recv()

        run(1, 16, arrival)
        total = dst[0]
        for p in range(1, 16):
            total = total + dst[p]
        return total

    gather(
        part_b, gather_b, b_send, b_recv, 1, project(jnp.concatenate([in1 * target1, hold1 * bar1], axis=0), 1)
    )
    discounting(2, 4)
    node_total = node_sum(ex0 * bar0, 0) + node_sum(ex1 * bar1, 1)

    @pl.when(owns[1])
    def _():
        answer = solve(gathered(part_b, gather_b, b_send, b_recv))
        answer_src[...] = answer
        answer_b[mine] = answer
        broadcast(answer_b, bb_send, bb_recv, mine)

    for g in range(4):
        collect(answer_b, bb_send, bb_recv, g, owner_of(1, g))
    coef1 = pick(answer_b, 0, 0)
    back1 = pick(answer_b, 0, 1)
    coefficient_out[1] = coef1
    values1 = ex1 * payoff_of(1) + hold1 * fit(coef1, 1) + out1 * target1
    target0 = discount[0:1, :] * values1
    gather(part_c, gather_c, c_send, c_recv, 0, project(jnp.concatenate([in0 * target0, zero4], axis=0), 0))

    bar2 = discount[1:2, :] * (out1 * bar1 + in1 * fit(back1, 1))
    node_total = node_total + node_sum(ex2 * bar2, 2)
    node_one[me] = jnp.concatenate([node_total[:, 128 * k : 128 * k + 128] for k in range(8)], axis=0)

    def one_copy(k):
        return remote(
            node_one.at[me], node_one.at[me], n1_send.at[k - 1], n1_recv.at[me], path_id((me + k) % 16)
        )

    def one_arrival(k):
        p = (me + k) % 16
        return remote(node_one.at[me], node_one.at[p], n1_send.at[0], n1_recv.at[p], path_id(p))

    def two_copy(k):
        return remote(
            node_two.at[tme], node_two.at[tme], n2_send.at[k - 1], n2_recv.at[tme], trade_id((tme + k) % 8)
        )

    def two_arrival(k):
        t = (tme + k) % 8
        return remote(node_two.at[tme], node_two.at[t], n2_send.at[0], n2_recv.at[t], trade_id(t))

    run(1, 16, lambda k: one_copy(k).start())

    @pl.when(owns[0])
    def _():
        answer = solve(gathered(part_c, gather_c, c_send, c_recv))
        broadcast_done(answer_a, a_send, a_recv, 4 + mine)
        answer_src[...] = answer
        answer_c[mine] = answer
        broadcast(answer_c, cc_send, cc_recv, mine)

    run(1, 16, lambda k: one_arrival(k).wait_recv())
    total = node_one[0]
    for p in range(1, 16):
        total = total + node_one[p]
    node_two[tme] = total
    run(1, 8, lambda k: two_copy(k).start())

    for g in range(4):
        collect(answer_c, cc_send, cc_recv, g, owner_of(0, g))
    coef0 = pick(answer_c, 0, 0)
    coefficient_out[0] = coef0
    values_out[...] = ex0 * payoff_of(0) + hold0 * fit(coef0, 0) + out0 * target0

    run(1, 8, lambda k: two_arrival(k).wait_recv())
    total = node_two[0]
    for t in range(1, 8):
        total = total + node_two[t]
    grid = (
        lax.broadcasted_iota(jnp.int32, (8, 128), 0) * 128 + lax.broadcasted_iota(jnp.int32, (8, 128), 1)
    ).astype(F32)
    adjoint = -((grid + 1.0) * (horizon / NODES)) * total
    node_out[...] = adjoint
    load_other(1).wait()
    line = jnp.concatenate([adjoint[k : k + 1, :] for k in range(8)], axis=1)
    bucket_out[...] = dot(jnp.broadcast_to(line, (8, NODES)), bucket_map[...], NT, HIGH)

    for i in (0, 2, 4):
        owner_copy(i).wait_send()
    for i in (1, 3, 5):

        @pl.when(z != owner_z(DATES[i // 2], yh, core))
        def _():
            owner_copy(i).wait_send()

    gather_sent(part_b, gather_b, b_send, b_recv, 1)
    gather_sent(part_c, gather_c, c_send, c_recv, 0)

    @pl.when(owns[2])
    def _():
        broadcast_done(answer_a, a_send, a_recv, mine)

    @pl.when(owns[1])
    def _():
        broadcast_done(answer_b, bb_send, bb_recv, mine)

    @pl.when(owns[0])
    def _():
        broadcast_done(answer_c, cc_send, cc_recv, mine)

    run(1, 16, lambda k: one_copy(k).wait_send())
    run(1, 8, lambda k: two_copy(k).wait_send())


def finish(values, coefficients, node, bucketed, values_out, coefficients_out, node_out, bucketed_out):
    values_out[...] = values[...]
    coefficients_out[...] = coefficients[...]
    node_out[...] = node[...].reshape(NODES)
    bucketed_out[...] = bucketed[0:1, :].reshape(64)


def shards(
    state,
    basis_projection_weight,
    factor_node_loading,
    curve,
    discount,
    region,
    carry_in,
    group_of,
    swap_start,
    swap_length,
    strike,
    notional,
    bucket_map,
):
    vmem = pl.BlockSpec(memory_space=pltpu.VMEM)
    anywhere = pl.BlockSpec(memory_space=pl.ANY)
    dma = pltpu.SemaphoreType.DMA
    values, coefficients, node, bucketed = pl.pallas_call(
        kernel,
        out_shape=(
            jax.ShapeDtypeStruct((GRP, LOCAL), F32),
            jax.ShapeDtypeStruct((EXD, GRP, BASIS), F32),
            jax.ShapeDtypeStruct((8, 128), F32),
            jax.ShapeDtypeStruct((8, 64), F32),
        ),
        in_specs=[anywhere, vmem, anywhere, *[vmem] * 9, anywhere],
        out_specs=(vmem,) * 4,
        scratch_shapes=[
            pltpu.VMEM((EXD, BASIS, LOCAL), BF16),
            pltpu.VMEM((EXD, 8, BASIS), F32),
            pltpu.VMEM((6, ROWS, 128), F32),
            pltpu.VMEM((6, ROWS, 128), F32),
            pltpu.VMEM((6, ROWS, 128), F32),
            pltpu.VMEM((8, ROWS, 128), F32),
            pltpu.VMEM((EXD * LOCAL, FAC), BF16),
            pltpu.VMEM((FAC, NODES), BF16),
            pltpu.VMEM((64, NODES), F32),
            pltpu.VMEM((EXD * LOCAL, NODES), BF16),
            pltpu.VMEM((EXD * LOCAL, NODES), BF16),
            pltpu.VMEM((8, TPAD), jnp.int32),
            pltpu.VMEM((8, TPAD), F32),
            pltpu.VMEM((12, GRP, 256), F32),
            pltpu.VMEM((BASIS, BASIS), F32),
            pltpu.VMEM((2, BASIS), F32),
            pltpu.VMEM((8, 2, BASIS), F32),
            pltpu.VMEM((4, 2, BASIS), F32),
            pltpu.VMEM((4, 2, BASIS), F32),
            pltpu.VMEM((4, 2, BASIS), F32),
            pltpu.VMEM((4, 2, BASIS), F32),
            pltpu.VMEM((16, 2, BASIS), F32),
            pltpu.VMEM((16, 2, BASIS), F32),
            pltpu.VMEM((16, 8, 128), F32),
            pltpu.VMEM((8, 8, 128), F32),
            dma((6,)),
            dma((6,)),
            dma((6,)),
            dma((8,)),
            dma((5,)),
            dma((15,)),
            dma((8,)),
            dma((4,)),
            dma((16,)),
            dma((15,)),
            dma((4,)),
            dma((4,)),
            dma((16,)),
            dma((15,)),
            dma((4,)),
            dma((15,)),
            dma((16,)),
            dma((7,)),
            dma((8,)),
        ],
        compiler_params=pltpu.CompilerParams(collective_id=0, has_side_effects=True),
        name="backward_window",
    )(
        state.reshape(EXD * LOCAL, FAC),
        basis_projection_weight,
        factor_node_loading,
        curve.reshape(1, NODES),
        discount,
        region.transpose(0, 2, 1),
        carry_in.T,
        group_of,
        swap_start,
        swap_length,
        strike,
        notional,
        bucket_map.T,
    )
    values, coefficients, node, bucketed = pl.pallas_call(
        finish,
        out_shape=(
            jax.ShapeDtypeStruct((GRP, LOCAL), F32),
            jax.ShapeDtypeStruct((EXD, GRP, BASIS), F32),
            jax.ShapeDtypeStruct((NODES,), F32),
            jax.ShapeDtypeStruct((64,), F32),
        ),
        in_specs=[vmem] * 4,
        out_specs=(vmem,) * 4,
        name="finish",
    )(values, coefficients, node, bucketed)
    return (values.T, coefficients, node, bucketed)


def solution(mesh):
    torus = Mesh(
        mesh.devices.reshape(2, 4, 2, 2, 4), ("path_0", "path_1", "path_2", "trade_0", "trade_1")
    )
    in_specs = (
        P(None, PATH, None),
        P(),
        P(),
        P(),
        P(None, PATH),
        P(None, PATH, TRADE),
        P(PATH, TRADE),
        P(TRADE),
        P(TRADE),
        P(TRADE),
        P(TRADE),
        P(TRADE),
        P(),
    )
    out_specs = (P(PATH, TRADE), P(None, TRADE, None), P(), P())
    return jax.shard_map(
        shards, mesh=torus, in_specs=in_specs, out_specs=out_specs, check_vma=False
    )
```
